32 devices in a mesh: slab: 8 (over z, y), grp: 4 (over x, core).
Axes of the slice: x: 2, y: 2, z: 4, core: 2. Of those that a mesh axis runs over, the one named last changes fastest.
Arguments:
- potential: bfloat16 [64, 8, 1024], P('slab'), may hold values from -3 to 3
- coefficients: bfloat16 [128, 16, 8, 1024], P(('slab', 'grp')), may hold values from -1 to 1
- box_center: int32 [128], replicated, may hold values from 0 to 63, as said below
- box_extent: int32 [128], replicated, may hold values from 8 to 16
Outputs:
- margin: float32 [128, 80], P(('slab', 'grp'))
- hamiltonian: float32 [128, 80], P(('slab', 'grp'))
The draws below stay inside these ranges and needn't reach their ends.
Inputs may be any that keep to these rules, and one draw needn't show every extreme that they name: `box_center`: function b's centre lies among the 8 planes of slab b // 16, that is from (8 * (b // 16)) on.
All inputs are finite; a program needn't handle non-finite values.
Results may differ from the reference program's by a relative error of at most 0.0003.
Values may be sent and summed in bfloat16 or wider, within the bound.
A program may use at most 64 MiB of HBM per device.

```python
import jax
import jax.numpy as jnp
from jax import lax

SZ = 8
EMAX = 16
COMP = 8
CX = 32
CY = 32
HW = 8
CS = 1024
NZ = 64
MEMBERS = 16
FUNCS = 128
BAND = 80
N_SLAB = 8


def draw_coefficients(key, part):
    keys = jax.random.split(jax.random.fold_in(key, 17), 3)
    centre_x = jax.random.uniform(keys[0], (FUNCS, 1), minval=0.0, maxval=float(CX))
    centre_y = jax.random.uniform(keys[1], (FUNCS, 1), minval=0.0, maxval=float(CY))
    cells = jnp.arange(CX * CY)
    cell_x = (cells // CY).astype(jnp.float32)[None, :]
    cell_y = (cells % CY).astype(jnp.float32)[None, :]
    delta_x = cell_x - centre_x
    delta_y = cell_y - centre_y
    envelope = 0.05 + jnp.exp(-(delta_x * delta_x + delta_y * delta_y) / 4.5)
    energy = jnp.sum(envelope * envelope, axis=1, keepdims=True)
    amplitude = 1.0 / jnp.sqrt(energy * float(EMAX * COMP))
    shape = (FUNCS, EMAX, COMP, CX * CY)
    base = jax.random.truncated_normal(keys[2], -6.0, 6.0, shape)
    values = base * (amplitude * envelope)[:, None, None, :]
    return values.astype(jnp.bfloat16)


def draw_box_center(key, part):
    offsets = jax.random.randint(jax.random.fold_in(key, 29), (FUNCS,), 0, SZ)
    owner = jnp.arange(FUNCS, dtype=jnp.int32) // (FUNCS // N_SLAB)
    return (owner * SZ + offsets).astype(jnp.int32)


def plant(array, own_key, low, largest):
    index_at = [jax.random.randint(jax.random.fold_in(own_key, axis), (), 0, length) for axis, length in enumerate(array.shape)]
    widest = array.shape.index(max(array.shape))
    next_to = index_at[:widest] + [(index_at[widest] + 1) % array.shape[widest]] + index_at[widest + 1:]
    return array.at[tuple(index_at)].set(low).at[tuple(next_to)].set(largest)


def levels(stream_key, dims, cuts, smallest, largest):
    def one(axis_at, blocks):
        draws = jax.random.uniform(jax.random.fold_in(jax.random.fold_in(stream_key, 6), axis_at), (blocks,), jnp.float32, smallest / len(cuts), largest / len(cuts))
        return jnp.repeat(jnp.exp(draws), dims[axis_at] // blocks).reshape((-1,) + (1,) * (len(dims) - axis_at - 1))

    loudness = one(*cuts[0])
    for cut in cuts[1:]:
        loudness = loudness * one(*cut)
    return loudness


def setup_inputs(seed: int = 0) -> dict:
    key_of = jax.random.split(jax.random.key(seed), 5)
    return {
        "potential": jnp.clip(jax.random.uniform(key_of[0], (NZ, COMP, CS), jnp.float32, -3.0, 3.0) * levels(key_of[0], (NZ, COMP, CS), ((0, 8),), -0.4, 0.0), -3.0, 3.0).astype(jnp.bfloat16),
        "coefficients": draw_coefficients(jax.random.fold_in(key_of[4], 71), 0),
        "box_center": draw_box_center(jax.random.fold_in(key_of[4], 71), 0),
        "box_extent": plant(jax.random.randint(key_of[3], (FUNCS,), EMAX // 2, EMAX + 1), jax.random.fold_in(key_of[3], 1), EMAX // 2, EMAX).astype(jnp.int32),
    }


def haar_signs():
    row_ids = jnp.arange(COMP, dtype=jnp.int32)[:, None]
    col_ids = jnp.arange(COMP, dtype=jnp.int32)[None, :]
    common = jnp.bitwise_and(row_ids, col_ids)
    parity = (common % 2 + (common // 2) % 2 + (common // 4) % 2) % 2
    return (1 - 2 * parity).astype(jnp.float32)


def apply_hamiltonian(orbital, pot_box, inside):
    shaped = orbital.reshape(orbital.shape[:3] + (CX, CY))
    bordered = jnp.pad(shaped, ((0, 0), (0, 0), (0, 0), (1, 1), (1, 1)))
    beside_all = bordered[:, :, :, 2:, 1:-1] + bordered[:, :, :, :-2, 1:-1] + bordered[:, :, :, 1:-1, 2:] + bordered[:, :, :, 1:-1, :-2]
    plane_term = (2.0 * shaped - 0.5 * beside_all).reshape(orbital.shape)
    padded = jnp.pad(orbital, ((0, 0), (1, 1), (0, 0), (0, 0)))
    depth_term = orbital - 0.5 * (padded[:, :-2] + padded[:, 2:])
    haar_table = haar_signs()
    fine_values = jnp.einsum("kc,npcx->npkx", haar_table, orbital, precision=lax.Precision.HIGHEST)
    potential_term = jnp.einsum("kc,npkx->npcx", haar_table, pot_box * fine_values, precision=lax.Precision.HIGHEST) / COMP
    return jnp.where(inside, plane_term + depth_term + potential_term, 0.0).astype(jnp.bfloat16)


def place_planes(starts, frame_depth, tile_data):
    source = jnp.arange(EMAX, dtype=jnp.int32)
    target = jnp.arange(frame_depth, dtype=jnp.int32)
    onehot = (starts[:, None, None] + source[None, None, :] == target[None, :, None]).astype(jnp.float32)
    return jnp.einsum("nqp,npcx->nqcx", onehot, tile_data, precision=lax.Precision.HIGHEST)


def reference(potential, coefficients, box_center, box_extent):
    frame_depth = SZ + EMAX
    planes = jnp.arange(EMAX, dtype=jnp.int32)
    member_ids = jnp.arange(MEMBERS, dtype=jnp.int32)
    steps_away = jnp.arange(5, dtype=jnp.int32) - 2

    def per_slab(slab_index):
        band_slabs = (slab_index + steps_away) % N_SLAB
        band_rows = (band_slabs[:, None] * MEMBERS + member_ids[None, :]).reshape(-1)
        centers = jnp.take(box_center, band_rows)
        extents = jnp.take(box_extent, band_rows)
        shifts = jnp.repeat(steps_away, MEMBERS, total_repeat_length=BAND)
        home = jnp.repeat(band_slabs, MEMBERS, total_repeat_length=BAND)
        relative = centers - home * SZ + shifts * SZ - extents // 2 + HW
        inside = planes[None, :] < extents[:, None]
        values = jnp.take(coefficients, band_rows, axis=0).astype(jnp.float32)
        orbital = jnp.where(inside[:, :, None, None], values, 0.0)
        window = place_planes(relative, frame_depth, orbital)
        own_orbital = orbital[2 * MEMBERS:3 * MEMBERS]
        own_relative = relative[2 * MEMBERS:3 * MEMBERS]
        own_inside = inside[2 * MEMBERS:3 * MEMBERS]
        plane_ids = (slab_index * SZ + own_relative - HW)[:, None] + planes[None, :]
        pot_box = jnp.take(potential, plane_ids % NZ, axis=0).astype(jnp.float32)
        applied = apply_hamiltonian(own_orbital, pot_box, own_inside[:, :, None, None])
        applied_window = place_planes(own_relative, frame_depth, applied.astype(jnp.float32))
        flat_window = window.reshape(window.shape[0], -1)
        own_window = window[2 * MEMBERS:3 * MEMBERS].reshape(MEMBERS, -1)
        margin_rows = jnp.dot(own_window, flat_window.T, precision=lax.Precision.HIGHEST)
        ham_rows = jnp.dot(applied_window.reshape(MEMBERS, -1), flat_window.T, precision=lax.Precision.HIGHEST)
        return margin_rows, ham_rows

    margin, hamiltonian = lax.map(per_slab, jnp.arange(N_SLAB, dtype=jnp.int32))
    return margin.reshape(FUNCS, BAND), hamiltonian.reshape(FUNCS, BAND)
```

```python
import functools

import jax
import jax.numpy as jnp
import numpy as np
from jax import lax
from jax.experimental import pallas as pl
from jax.experimental.pallas import tpu as pltpu
from jax.sharding import PartitionSpec as P

COMP = 8
CX = 32
CY = 32
BLOCK = 256
LANES = 128
MESH = pl.DeviceIdType.MESH
PAIRS = ((0, 3), (1, 2))
SHORT = (0, 3, 1, 2)


def haar_signs():
    ids = np.arange(COMP)
    common = ids[:, None] & ids[None, :]
    parity = (common % 2 + common // 2 % 2 + common // 4 % 2) % 2
    return (1 - 2 * parity).astype(np.float32)


def matrices(rows):
    haar = np.einsum("kc,mn->kmnc", haar_signs(), np.eye(rows, dtype=np.float32))
    haar = haar.reshape(COMP * rows, rows * COMP)
    lap = np.zeros((BLOCK, BLOCK), np.float32)
    for i in range(BLOCK):
        if i % CY:
            lap[i - 1, i] = lap[i, i - 1] = -0.5
        if i >= CY:
            lap[i - CY, i] = lap[i, i - CY] = -0.5
    return jnp.asarray(haar, jnp.bfloat16), jnp.asarray(lap, jnp.bfloat16)


def band_kernel(
    slabs,
    groups,
    depth,
    pot_ref,
    center_ref,
    extent_ref,
    haar_ref,
    lap_ref,
    coef_hbm,
    out_ref,
    coef,
    frames,
    raw,
    far,
    orb,
    rest,
    pot,
    pot_out,
    pot_in,
    limits,
    acc,
    place,
    rows,
    got_rows,
    load_sem,
    pot_send,
    pot_recv,
    tile_send,
    tile_recv,
    far_send,
    far_recv,
    rows_send,
    rows_recv,
):
    f32, bf16 = jnp.float32, jnp.bfloat16
    slab = lax.axis_index("slab")
    me = lax.axis_index("grp")
    per, box, comp, cells = coef.shape
    half = depth // 2
    team = 2 * groups
    rows_tile = 4 * per
    odd = lax.rem(slab, 2)
    base = slab - odd
    mine = odd * groups + me
    ahead = lax.rem(slab + 2, slabs)
    behind = lax.rem(slab + slabs - 2, slabs)

    def mate(step):
        low, scale, rest_of, bits = 0, 1, me, step
        while scale < groups:
            bit = lax.rem(rest_of, 2)
            rest_of = rest_of // 2
            low = low + scale * (1 - bit if bits % 2 else bit)
            bits //= 2
            scale *= 2
        par = 1 - odd if bits else odd
        return par, low

    steps = [6, 2, 4, 7, 3, 5, 1, 0] if groups == 4 else list(range(team - 1, -1, -1))

    loads = [
        pltpu.make_async_copy(coef_hbm.at[f], coef.at[f], load_sem.at[f]) for f in range(per)
    ]
    for copy in loads:
        copy.start()

    barrier = pltpu.get_barrier_semaphore()
    for step in steps:
        if step:
            par, low = mate(step)
            pl.semaphore_signal(
                barrier, inc=1, device_id=(base + par, low), device_id_type=MESH
            )
    for place_at in (ahead, behind):
        pl.semaphore_signal(barrier, inc=1, device_id=(place_at, me), device_id_type=MESH)

    unsent = []

    def push(source, target, send, recv, to):
        copy = pltpu.make_async_remote_copy(
            src_ref=source,
            dst_ref=target,
            send_sem=send,
            recv_sem=recv,
            device_id=to,
            device_id_type=MESH,
        )
        copy.start()
        unsent.append(copy)
        return copy

    def arrive(block, sem):
        pltpu.make_async_copy(block, block, sem).wait()

    def iota(shape, dim):
        return lax.broadcasted_iota(jnp.int32, shape, dim)

    def plane_of(row):
        pair = row // 8
        first = jnp.where(pair == 1, 3, jnp.where(pair == 2, 1, jnp.where(pair == 3, 2, 0)))
        return first + half * (lax.rem(row, 8) // per)

    theirs = (1 - odd) * groups + me
    own_pot = pot_ref[...].astype(f32).reshape(depth * comp, cells).astype(bf16)
    at_plane, at_column = iota((16, depth * comp), 0), iota((16, depth * comp), 1)
    pick = jnp.where(at_column == at_plane * comp + theirs, 1.0, 0.0).astype(bf16)
    sent = jnp.dot(pick, own_pot, preferred_element_type=f32)
    pot_out[...] = sent[:depth].astype(bf16)
    at_row, at_column = iota((4 * depth, depth * comp), 0), iota((4 * depth, depth * comp), 1)
    pick = jnp.where(at_column == plane_of(at_row) * comp + mine, 1.0, 0.0).astype(bf16)
    pot[odd] = jnp.dot(pick, own_pot, preferred_element_type=f32)

    row8 = iota((8, LANES), 0)
    func = lax.rem(row8, per)
    upper = row8 // per

    def spread(values):
        vec = jnp.full((8, LANES), values[0], jnp.int32)
        for f in range(1, per):
            vec = jnp.where(func == f, values[f], vec)
        return vec

    first = (slab * groups + me) * per
    extents = [extent_ref[first + f] for f in range(per)]
    starts = [
        center_ref[first + f] - slab * depth - lax.shift_right_logical(extents[f], 1)
        for f in range(per)
    ]
    start_rows, end_rows = spread(starts), spread([s + e for s, e in zip(starts, extents)])

    def build(index, outer, pairs):
        planes, masks = [], []
        for i in pairs:
            for h in range(2):
                for f in range(per):
                    j = i + half * h
                    if outer:
                        p = j + depth - starts[f]
                        p = jnp.where(p < extents[f], p, p - 2 * depth)
                    else:
                        p = j - starts[f]
                    planes.append(coef[f, jnp.clip(p, 0, box - 1)].astype(f32))
            j = i + half * upper
            if outer:
                masks.append((j < end_rows - depth) | (j >= start_rows + depth))
            else:
                masks.append((j >= start_rows) & (j < end_rows))
        stacked = jnp.concatenate(planes, 0).astype(bf16)
        fine = jnp.dot(haar_ref[...], stacked, preferred_element_type=f32)
        keep = jnp.concatenate(masks, 0)
        for k in range(comp):
            for v in range(cells // LANES):
                at = slice(v * LANES, (v + 1) * LANES)
                part = fine[k * rows_tile : (k + 1) * rows_tile, at]
                frames[index, k, :, at] = jnp.where(keep, part, 0.0).astype(bf16)

    def tile_target(index, par, low):
        if index in (0, 3):
            return orb.at[par, index // 3, (1 + par) * groups + low]
        return raw.at[index - 1, par * groups + low]

    def send_tiles(index):
        for step in steps:
            par, low = mate(step)
            source = frames.at[index, par * groups + low]
            target = tile_target(index, odd, me)
            recv = tile_recv.at[index, mine]
            if step:
                push(source, target, tile_send.at[index, step], recv, (base + par, low))
            else:
                pltpu.make_async_copy(source, target, recv).start()

    pl.semaphore_wait(barrier, team + 1)
    push(pot_out, pot_in, pot_send, pot_recv, (base + 1 - odd, me))
    for copy in loads:
        copy.wait()
    build(0, False, PAIRS[0])
    send_tiles(0)
    build(1, True, PAIRS[0])
    send_tiles(1)
    build(2, True, PAIRS[1])
    send_tiles(2)
    build(3, False, PAIRS[1])
    send_tiles(3)

    for slot in range(4):
        home = lax.rem(base + slabs - 1 + slot, slabs)
        for g in range(groups):
            at = (home * groups + g) * per
            ext = [extent_ref[at + f] for f in range(per)]
            begin = [
                center_ref[at + f] - home * depth - lax.shift_right_logical(ext[f], 1)
                for f in range(per)
            ]
            limits[slot, g, 0] = spread(begin)
            limits[slot, g, 1] = spread([b + e for b, e in zip(begin, ext)])

    at_row, at_column = iota((2 * LANES, LANES), 0), iota((2 * LANES, LANES), 1)
    lane = lax.rem(at_row, LANES)
    slot_of = lane // 64 + 2 * (lax.rem(lane, 8 * 2) // 8)
    member = lax.rem(lane, 64) // 16 * per + lax.rem(lane, 8)
    near = at_row < LANES
    band = jnp.where(near, slot_of + 1 - odd, slot_of - 1 + 3 * odd)
    fits = (lax.rem(lane, 8) < per) & (band >= 0) & (band < 5)
    fits = fits & (at_column == band * groups * per + member)
    place[...] = jnp.where(fits, 1.0, 0.0)

    arrive(pot_in, pot_recv)
    padded = jnp.concatenate([pot_in[...].astype(f32), jnp.zeros((depth, cells), f32)], 0)
    at_row, at_column = iota((4 * depth, 2 * depth), 0), iota((4 * depth, 2 * depth), 1)
    pick = jnp.where(at_column == plane_of(at_row), 1.0, 0.0).astype(bf16)
    pot[1 - odd] = jnp.dot(pick, padded.astype(bf16), preferred_element_type=f32)

    for index in range(3):
        for step in steps:
            par, low = mate(step)
            block = tile_target(index, par, low)
            arrive(block, tile_recv.at[index, par * groups + low])
            to = lax.rem(slab + slabs + 4 * par - 2, slabs)
            push(
                block,
                far.at[1 - par, index, low],
                far_send.at[index, step],
                far_recv.at[1 - par, index, low],
                (to, me),
            )

    low_half = row8 < per
    lane8 = iota((8, LANES), 1)
    vregs = cells // LANES
    blocks = cells // BLOCK
    per_block = BLOCK // LANES

    def load(ref, top):
        wide = ref[top : top + 8].astype(f32)
        return [wide[:, v * LANES : (v + 1) * LANES] for v in range(vregs)]

    def swap(low_rows, high_rows):
        return [
            pltpu.roll(jnp.where(low_half, a, b), per, 0) for a, b in zip(low_rows, high_rows)
        ]

    def select(keep, rows_in):
        return [jnp.where(keep, x, 0.0) for x in rows_in]

    def split(ref):
        wide = ref[...].astype(f32)
        cut = lambda part: [part[:, v * LANES : (v + 1) * LANES] for v in range(vregs)]
        return cut(wide[:8]), cut(wide[8:])

    def finish(side, at, planes, before, after, keeps):
        tiles = [orb.at[side, t, at] for t in range(2)]
        stack = []
        for q in range(blocks):
            for t in range(2):
                stack.append(tiles[t][:, q * BLOCK : (q + 1) * BLOCK])
        beside = jnp.dot(jnp.concatenate(stack, 0), lap_ref[...], preferred_element_type=f32)
        shifted = [before, *planes, after]
        for v in range(vregs):
            done = {}
            q, part = divmod(v, per_block)
            for n, i in enumerate(SHORT):
                total = shifted[i][v] + shifted[i + 2][v]
                if part == 0 and v:
                    moved = pltpu.roll(planes[i][v - 1], CY, 1)
                    total = total + jnp.where(lane8 < CY, moved, 0.0)
                if part == per_block - 1 and v < vregs - 1:
                    moved = pltpu.roll(planes[i][v + 1], LANES - CY, 1)
                    total = total + jnp.where(lane8 >= LANES - CY, moved, 0.0)
                top = (q * 4 + n) * 8
                value = beside[top : top + 8, part * LANES : (part + 1) * LANES]
                value = value - 0.5 * total
                value = value + pot[side, n * 8 : n * 8 + 8, v * LANES : (v + 1) * LANES] * (
                    planes[i][v]
                )
                done[i] = jnp.where(keeps[i], value, 0.0)
            for t in range(2):
                both = jnp.concatenate([done[i] for i in PAIRS[t]], 0)
                rest[side, t, at, :, v * LANES : (v + 1) * LANES] = both.astype(bf16)

    def outer_frame(side, at, slot, g, up, main_tile, first_tile, second_tile):
        begin, end = limits[slot, g, 0], limits[slot, g, 1]
        if up:
            keeps = [i + half * upper < end - depth for i in range(half)]
        else:
            keeps = [i + half * upper >= begin + depth for i in range(half)]
        p0, p3 = split(first_tile)
        p1, p2 = split(second_tile)
        planes = [select(keeps[i], p) for i, p in enumerate((p0, p1, p2, p3))]
        for v in range(vregs):
            for t in range(2):
                both = jnp.concatenate([planes[i][v] for i in PAIRS[t]], 0)
                orb[side, t, at, :, v * LANES : (v + 1) * LANES] = both.astype(bf16)
        main0, main3 = split(main_tile)
        zero = [jnp.zeros((8, LANES), f32)] * vregs
        if up:
            before, after = swap(planes[3], main3), swap(zero, planes[0])
        else:
            before, after = swap(planes[3], zero), swap(main0, planes[0])
        finish(side, at, planes, before, after, keeps)

    def main_frame(side, at, slot, g, outer_tile):
        begin, end = limits[slot, g, 0], limits[slot, g, 1]
        keeps = [
            (i + half * upper >= begin) & (i + half * upper < end) for i in range(half)
        ]
        p0, p3 = split(orb.at[side, 0, at])
        p1, p2 = split(orb.at[side, 1, at])
        planes = [p0, p1, p2, p3]
        out0, out3 = split(outer_tile)
        down3 = select(half - 1 + half * upper >= begin + depth, out3)
        up0 = select(half * upper < end - depth, out0)
        finish(side, at, planes, swap(p3, down3), swap(up0, p0), keeps)

    @pl.loop(0, groups)
    def _(g):
        outer_frame(
            1, groups + g, 1, g, True, orb.at[0, 0, groups + g], raw.at[0, g], raw.at[1, g]
        )
        outer_frame(
            0,
            2 * groups + g,
            2,
            g,
            False,
            orb.at[1, 0, 2 * groups + g],
            raw.at[0, groups + g],
            raw.at[1, groups + g],
        )

    for index in range(3):
        for side in range(2):
            for g in range(groups):
                arrive(far.at[side, index, g], far_recv.at[side, index, g])

    @pl.loop(0, groups)
    def _(g):
        outer_frame(0, g, 0, g, True, far.at[0, 0, g], far.at[0, 1, g], far.at[0, 2, g])
        outer_frame(1, g, 3, g, False, far.at[1, 0, g], far.at[1, 1, g], far.at[1, 2, g])

    for step in steps:
        par, low = mate(step)
        arrive(tile_target(3, par, low), tile_recv.at[3, par * groups + low])

    @pl.loop(0, groups)
    def _(g):
        main_frame(0, groups + g, 1, g, raw.at[0, g])
        main_frame(1, 2 * groups + g, 2, g, raw.at[0, groups + g])

    count = 3 * groups
    wide = count * rows_tile
    for side in range(2):
        for t in range(2):
            columns = orb[side, t].reshape(wide, cells)
            images = rest[side, t].reshape(wide, cells)
            full = jnp.concatenate([columns, columns[: 2 * LANES - wide]], 0)
            part = lax.dot_general(
                jnp.concatenate([columns, images], 0),
                full,
                (((1,), (1,)), ((), ())),
                preferred_element_type=f32,
            )
            if t:
                acc[side] += part
            else:
                acc[side] = part

    quarter = lax.rem(lane8, 16) // per
    own_plane = [quarter == upper + 2 * pi for pi in range(2)]

    def gathered(side, at):
        both = []
        for kind in range(2):
            top = (kind * count + at) * rows_tile
            parts = []
            for v in range(2):
                lanes = slice(v * LANES, (v + 1) * LANES)
                value = jnp.where(own_plane[0], acc[side, top : top + 8, lanes], 0.0)
                value += jnp.where(own_plane[1], acc[side, top + 8 : top + 16, lanes], 0.0)
                value += pltpu.roll(value, per, 0)
                value += pltpu.roll(value, LANES - 4, 1)
                value += pltpu.roll(value, LANES - 8, 1)
                parts.append(value)
            both.append(parts)
        return [jnp.where(low_half, both[0][v], both[1][v]) for v in range(2)]

    left = lane8 < LANES // 2
    even = lax.rem(lane8, 16) < 8
    zero = jnp.zeros((8, LANES), f32)
    for slot in (3, 0, 1, 2):
        for g in range(groups):
            v0, v1 = gathered(0, slot * groups + g) if slot < 3 else (zero, zero)
            w0, w1 = gathered(1, slot % 3 * groups + g) if slot else (zero, zero)
            near_cols = jnp.where(left, v0, v0 + w0)
            far_cols = jnp.where(left, v1 + w1, pltpu.roll(w0, LANES // 2, 1))
            if slot == 3:
                near_cols = jnp.where(left, 0.0, w0)
            rows[slot, g] = jnp.where(even, near_cols, pltpu.roll(far_cols, 8, 1))

    for slot in (3, 0):
        to = lax.rem(base + slabs - 1 + slot, slabs)
        for g in range(groups):
            push(
                rows.at[slot, g],
                got_rows.at[1, mine],
                rows_send.at[slot, g],
                rows_recv.at[1, mine],
                (to, g),
            )
    for step in steps:
        par, low = mate(step)
        source, target = rows.at[1 + par, low], got_rows.at[0, mine]
        if step:
            push(source, target, rows_send.at[1, step], rows_recv.at[0, mine], (base + par, low))
        else:
            pltpu.make_async_copy(source, target, rows_recv.at[0, mine]).start()
    for side in range(2):
        for r in range(team):
            arrive(got_rows.at[side, r], rows_recv.at[side, r])
    sums = []
    for side in range(2):
        total = got_rows[side, 0]
        for r in range(1, team):
            total = total + got_rows[side, r]
        sums.append(total)
    total = jnp.dot(
        jnp.concatenate(sums, 1),
        place[...],
        preferred_element_type=f32,
        precision=lax.Precision.HIGHEST,
    ) * (1.0 / comp)
    out_ref[...] = total + jnp.where(low_half, 0.0, 3.0 * pltpu.roll(total, per, 0))
    for copy in unsent:
        copy.wait_send()


def split_kernel(band_ref, margin_ref, ham_ref):
    per, width = margin_ref.shape
    margin_ref[...] = band_ref[:per, :width]
    ham_ref[...] = band_ref[per:, :width]


def local(slabs, groups, potential, coefficients, box_center, box_extent):
    per, box, comp, cells = coefficients.shape
    depth = potential.shape[0]
    team = 2 * groups
    rows_tile = 4 * per
    assert (depth, per, comp, groups) == (8, 4, team, 4)
    vmem = pl.BlockSpec(memory_space=pltpu.VMEM)
    smem = pl.BlockSpec(memory_space=pltpu.SMEM)
    anywhere = pl.BlockSpec(memory_space=pl.ANY)
    bf16, f32 = jnp.bfloat16, jnp.float32
    tiles = lambda *lead: pltpu.VMEM((*lead, rows_tile, cells), bf16)
    dma = pltpu.SemaphoreType.DMA
    band = pl.pallas_call(
        functools.partial(band_kernel, slabs, groups, depth),
        out_shape=jax.ShapeDtypeStruct((2 * per, LANES), f32),
        in_specs=[vmem, smem, smem, vmem, vmem, anywhere],
        out_specs=vmem,
        scratch_shapes=[
            pltpu.VMEM((per, box, comp, cells), bf16),
            tiles(4, comp),
            tiles(2, team),
            tiles(2, 3, groups),
            tiles(2, 2, 3 * groups),
            tiles(2, 2, 3 * groups),
            pltpu.VMEM((2, 4 * depth, cells), f32),
            pltpu.VMEM((depth, cells), bf16),
            pltpu.VMEM((depth, cells), bf16),
            pltpu.VMEM((4, groups, 2, 8, LANES), jnp.int32),
            pltpu.VMEM((2, 6 * groups * rows_tile, 2 * LANES), f32),
            pltpu.VMEM((2 * LANES, LANES), f32),
            pltpu.VMEM((4, groups, 2 * per, LANES), f32),
            pltpu.VMEM((2, team, 2 * per, LANES), f32),
            dma((per,)),
            dma,
            dma,
            dma((4, team)),
            dma((4, team)),
            dma((3, team)),
            dma((2, 3, groups)),
            dma((4, team)),
            dma((2, team)),
        ],
        compiler_params=pltpu.CompilerParams(collective_id=0, has_side_effects=True),
        name="band",
    )(potential, box_center, box_extent, *matrices(rows_tile), coefficients)
    out = jax.ShapeDtypeStruct((per, 5 * groups * per), f32)
    return pl.pallas_call(
        split_kernel, out_shape=(out, out), in_specs=[vmem], out_specs=(vmem, vmem), name="split"
    )(band)


def solution(mesh):
    return jax.shard_map(
        functools.partial(local, mesh.shape["slab"], mesh.shape["grp"]),
        mesh=mesh,
        in_specs=(P("slab", None, None), P(("slab", "grp"), None, None, None), P(), P()),
        out_specs=(P(("slab", "grp"), None), P(("slab", "grp"), None)),
        check_vma=False,
    )
```

```python
import functools

import jax
import jax.numpy as jnp
import numpy as np
from jax import lax
from jax.experimental import pallas as pl
from jax.experimental.pallas import tpu as pltpu
from jax.sharding import PartitionSpec as P

COMP = 8
CX = 32
CY = 32
BLOCK = 256
LANES = 128
MESH = pl.DeviceIdType.MESH
PAIRS = ((0, 3), (1, 2))
SHORT = (0, 3, 1, 2)


def haar_signs():
    ids = np.arange(COMP)
    common = ids[:, None] & ids[None, :]
    parity = (common % 2 + common // 2 % 2 + common // 4 % 2) % 2
    return (1 - 2 * parity).astype(np.float32)


def matrices(rows):
    haar = np.einsum("kc,mn->kmnc", haar_signs(), np.eye(rows, dtype=np.float32))
    haar = haar.reshape(COMP * rows, rows * COMP)
    lap = np.zeros((BLOCK, BLOCK), np.float32)
    for i in range(BLOCK):
        if i % CY:
            lap[i - 1, i] = lap[i, i - 1] = -0.5
        if i >= CY:
            lap[i - CY, i] = lap[i, i - CY] = -0.5
    return jnp.asarray(haar, jnp.bfloat16), jnp.asarray(lap, jnp.bfloat16)


def band_kernel(
    slabs,
    groups,
    depth,
    pot_hbm,
    center_hbm,
    extent_hbm,
    haar_hbm,
    lap_hbm,
    coef_hbm,
    out_ref,
    pot_ref,
    center_ref,
    extent_ref,
    haar_ref,
    lap_ref,
    coef,
    frames,
    raw,
    far,
    halo_out,
    halo_in,
    orb,
    rest,
    pot,
    pot_out,
    pot_in,
    limits,
    acc,
    place,
    rows,
    got_rows,
    load_sem,
    pot_send,
    pot_recv,
    tile_send,
    tile_recv,
    far_send,
    far_recv,
    halo_send,
    halo_recv,
    rows_send,
    rows_recv,
):
    f32, bf16 = jnp.float32, jnp.bfloat16
    slab = lax.axis_index("slab")
    me = lax.axis_index("grp")
    per, box, comp, cells = coef.shape
    half = depth // 2
    team = 2 * groups
    rows_tile = 4 * per
    odd = lax.rem(slab, 2)
    base = slab - odd
    mine = odd * groups + me
    ahead = lax.rem(slab + 2, slabs)
    behind = lax.rem(slab + slabs - 2, slabs)

    def mate(step):
        low, scale, rest_of, bits = 0, 1, me, step
        while scale < groups:
            bit = lax.rem(rest_of, 2)
            rest_of = rest_of // 2
            low = low + scale * (1 - bit if bits % 2 else bit)
            bits //= 2
            scale *= 2
        par = 1 - odd if bits else odd
        return par, low

    steps = [6, 2, 4, 7, 3, 5, 1, 0]

    loads = [
        pltpu.make_async_copy(source, target, load_sem.at[n])
        for n, (source, target) in enumerate(
            (
                (center_hbm, center_ref),
                (extent_hbm, extent_ref),
                (coef_hbm, coef),
                (haar_hbm, haar_ref),
                (pot_hbm, pot_ref),
                (lap_hbm, lap_ref),
            )
        )
    ]
    for copy in loads:
        copy.start()

    barrier = pltpu.get_barrier_semaphore()
    for step in steps:
        if step:
            par, low = mate(step)
            pl.semaphore_signal(
                barrier, inc=1, device_id=(base + par, low), device_id_type=MESH
            )
    for place_at in (ahead, behind):
        pl.semaphore_signal(barrier, inc=1, device_id=(place_at, me), device_id_type=MESH)

    unsent = []

    def push(source, target, send, recv, to):
        copy = pltpu.make_async_remote_copy(
            src_ref=source,
            dst_ref=target,
            send_sem=send,
            recv_sem=recv,
            device_id=to,
            device_id_type=MESH,
        )
        copy.start()
        unsent.append(copy)
        return copy

    def arrive(block, sem):
        pltpu.make_async_copy(block, block, sem).wait()

    def iota(shape, dim):
        return lax.broadcasted_iota(jnp.int32, shape, dim)

    def plane_of(row):
        pair = row // 8
        first = jnp.where(pair == 1, 3, jnp.where(pair == 2, 1, jnp.where(pair == 3, 2, 0)))
        return first + half * (lax.rem(row, 8) // per)

    row8 = iota((8, LANES), 0)
    func = lax.rem(row8, per)
    upper = row8 // per

    def spread(values):
        vec = jnp.full((8, LANES), values[0], jnp.int32)
        for f in range(1, per):
            vec = jnp.where(func == f, values[f], vec)
        return vec

    loads[0].wait()
    loads[1].wait()
    first = (slab * groups + me) * per
    extents = [extent_ref[first + f] for f in range(per)]
    starts = [
        center_ref[first + f] - slab * depth - lax.shift_right_logical(extents[f], 1)
        for f in range(per)
    ]
    start_rows, end_rows = spread(starts), spread([s + e for s, e in zip(starts, extents)])

    def build(index, outer, pairs):
        planes, masks = [], []
        for i in pairs:
            for h in range(2):
                for f in range(per):
                    j = i + half * h
                    if outer:
                        p = j + depth - starts[f]
                        p = jnp.where(p < extents[f], p, p - 2 * depth)
                    else:
                        p = j - starts[f]
                    planes.append(coef[f, jnp.clip(p, 0, box - 1)].astype(f32))
            j = i + half * upper
            if outer:
                masks.append((j < end_rows - depth) | (j >= start_rows + depth))
            else:
                masks.append((j >= start_rows) & (j < end_rows))
        stacked = jnp.concatenate(planes, 0).astype(bf16)
        fine = jnp.dot(haar_ref[...], stacked, preferred_element_type=f32)
        keep = jnp.concatenate(masks, 0)
        for k in range(comp):
            for v in range(cells // LANES):
                at = slice(v * LANES, (v + 1) * LANES)
                part = fine[k * rows_tile : (k + 1) * rows_tile, at]
                frames[index, k, :, at] = jnp.where(keep, part, 0.0).astype(bf16)

    def tile_target(index, par, low):
        if index in (0, 3):
            return orb.at[par, index // 3, (1 + par) * groups + low]
        return raw.at[index - 1, par * groups + low]

    def send_tiles(index):
        for step in steps:
            par, low = mate(step)
            source = frames.at[index, par * groups + low]
            target = tile_target(index, odd, me)
            recv = tile_recv.at[index, mine]
            if step:
                push(source, target, tile_send.at[index, step], recv, (base + par, low))
            else:
                pltpu.make_async_copy(source, target, recv).start()

    def relay(index, step):
        par, low = mate(step)
        if step:
            block = tile_target(index, par, low)
            arrive(block, tile_recv.at[index, par * groups + low])
        else:
            block = frames.at[index, mine]
        push(
            block,
            far.at[1 - par, index - 1, low],
            far_send.at[index - 1, step],
            far_recv.at[1 - par, index - 1, low],
            (lax.rem(slab + slabs + 4 * par - 2, slabs), me),
        )

    loads[2].wait()
    loads[3].wait()
    build(1, True, PAIRS[0])
    build(2, True, PAIRS[1])
    pl.semaphore_wait(barrier, team + 1)
    send_tiles(1)
    relay(1, 0)
    relay(2, 0)
    build(0, False, PAIRS[0])
    send_tiles(0)
    send_tiles(2)
    relay(1, 1)
    build(3, False, PAIRS[1])
    send_tiles(3)
    relay(2, 1)
    loads[4].wait()
    theirs = (1 - odd) * groups + me
    own_pot = pot_ref[...].astype(f32).reshape(depth * comp, cells).astype(bf16)
    at_plane, at_column = iota((16, depth * comp), 0), iota((16, depth * comp), 1)
    pick = jnp.where(at_column == at_plane * comp + theirs, 1.0, 0.0).astype(bf16)
    sent = jnp.dot(pick, own_pot, preferred_element_type=f32)
    pot_out[...] = sent[:depth].astype(bf16)
    at_row, at_column = iota((4 * depth, depth * comp), 0), iota((4 * depth, depth * comp), 1)
    pick = jnp.where(at_column == plane_of(at_row) * comp + mine, 1.0, 0.0).astype(bf16)
    pot[odd] = jnp.dot(pick, own_pot, preferred_element_type=f32)

    push(pot_out, pot_in, pot_send, pot_recv, (base + 1 - odd, me))

    for slot in range(4):
        home = lax.rem(base + slabs - 1 + slot, slabs)
        for g in range(groups):
            at = (home * groups + g) * per
            ext = [extent_ref[at + f] for f in range(per)]
            begin = [
                center_ref[at + f] - home * depth - lax.shift_right_logical(ext[f], 1)
                for f in range(per)
            ]
            limits[slot, g, 0] = spread(begin)
            limits[slot, g, 1] = spread([b + e for b, e in zip(begin, ext)])

    at_row, at_column = iota((2 * LANES, LANES), 0), iota((2 * LANES, LANES), 1)
    lane = lax.rem(at_row, LANES)
    slot_of = lane // 64 + 2 * (lax.rem(lane, 8 * 2) // 8)
    member = lax.rem(lane, 64) // 16 * per + lax.rem(lane, 8)
    near = at_row < LANES
    band = jnp.where(near, slot_of + 1 - odd, slot_of - 1 + 3 * odd)
    fits = (lax.rem(lane, 8) < per) & (band >= 0) & (band < 5)
    fits = fits & (at_column == band * groups * per + member)
    place[...] = jnp.where(fits, 1.0, 0.0)

    low_half = row8 < per
    lane8 = iota((8, LANES), 1)
    vregs = cells // LANES
    blocks = cells // BLOCK
    per_block = BLOCK // LANES

    def split(ref):
        wide = ref[...].astype(f32)
        cut = lambda part: [part[:, v * LANES : (v + 1) * LANES] for v in range(vregs)]
        return cut(wide[:8]), cut(wide[8:])

    for step in steps[:6]:
        relay(1, step)
    for step in steps:
        par, low = mate(step)
        arrive(tile_target(0, par, low), tile_recv.at[0, par * groups + low])
    for side in range(2):
        edges = [split(orb.at[side, 0, (1 + side) * groups + g])[side] for g in range(groups)]
        for n in range(groups // 2):
            one, two = edges[2 * n], edges[2 * n + 1]
            for v in range(vregs):
                if side:
                    both = jnp.where(low_half, pltpu.roll(one[v], per, 0), two[v])
                else:
                    both = jnp.where(low_half, one[v], pltpu.roll(two[v], per, 0))
                halo_out[side, 8 * n : 8 * n + 8, v * LANES : (v + 1) * LANES] = both.astype(bf16)
        push(
            halo_out.at[side],
            halo_in.at[1 - side],
            halo_send.at[side],
            halo_recv.at[1 - side],
            (ahead if side else behind, me),
        )
    for step in steps[:6]:
        relay(2, step)
    for index in (1, 2):
        arrive(tile_target(index, odd, me), tile_recv.at[index, mine])
    loads[5].wait()
    arrive(pot_in, pot_recv)
    padded = jnp.concatenate([pot_in[...].astype(f32), jnp.zeros((depth, cells), f32)], 0)
    at_row, at_column = iota((4 * depth, 2 * depth), 0), iota((4 * depth, 2 * depth), 1)
    pick = jnp.where(at_column == plane_of(at_row), 1.0, 0.0).astype(bf16)
    pot[1 - odd] = jnp.dot(pick, padded.astype(bf16), preferred_element_type=f32)

    def swap(low_rows, high_rows):
        return [
            pltpu.roll(jnp.where(low_half, a, b), per, 0) for a, b in zip(low_rows, high_rows)
        ]

    def select(keep, rows_in):
        return [jnp.where(keep, x, 0.0) for x in rows_in]

    def finish(side, at, planes, before, after, keeps):
        tiles = [orb.at[side, t, at] for t in range(2)]
        stack = []
        for q in range(blocks):
            for t in range(2):
                stack.append(tiles[t][:, q * BLOCK : (q + 1) * BLOCK])
        beside = jnp.dot(jnp.concatenate(stack, 0), lap_ref[...], preferred_element_type=f32)
        shifted = [before, *planes, after]
        for v in range(vregs):
            done = {}
            q, part = divmod(v, per_block)
            for n, i in enumerate(SHORT):
                total = shifted[i][v] + shifted[i + 2][v]
                if part == 0 and v:
                    moved = pltpu.roll(planes[i][v - 1], CY, 1)
                    total = total + jnp.where(lane8 < CY, moved, 0.0)
                if part == per_block - 1 and v < vregs - 1:
                    moved = pltpu.roll(planes[i][v + 1], LANES - CY, 1)
                    total = total + jnp.where(lane8 >= LANES - CY, moved, 0.0)
                top = (q * 4 + n) * 8
                value = beside[top : top + 8, part * LANES : (part + 1) * LANES]
                value = value - 0.5 * total
                value = value + pot[side, n * 8 : n * 8 + 8, v * LANES : (v + 1) * LANES] * (
                    planes[i][v]
                )
                done[i] = jnp.where(keeps[i], value, 0.0)
            for t in range(2):
                both = jnp.concatenate([done[i] for i in PAIRS[t]], 0)
                rest[side, t, at, :, v * LANES : (v + 1) * LANES] = both.astype(bf16)

    def outer_frame(side, at, slot, g, up, edge, first_tile, second_tile):
        begin, end = limits[slot, g, 0], limits[slot, g, 1]
        if up:
            keeps = [i + half * upper < end - depth for i in range(half)]
        else:
            keeps = [i + half * upper >= begin + depth for i in range(half)]
        p0, p3 = split(first_tile)
        p1, p2 = split(second_tile)
        planes = [select(keeps[i], p) for i, p in enumerate((p0, p1, p2, p3))]
        for v in range(vregs):
            for t in range(2):
                both = jnp.concatenate([planes[i][v] for i in PAIRS[t]], 0)
                orb[side, t, at, :, v * LANES : (v + 1) * LANES] = both.astype(bf16)
        zero = [jnp.zeros((8, LANES), f32)] * vregs
        if up:
            before, after = swap(planes[3], edge), swap(zero, planes[0])
        else:
            before, after = swap(planes[3], zero), swap(edge, planes[0])
        finish(side, at, planes, before, after, keeps)

    def main_frame(side, at, slot, g, outer_tile):
        begin, end = limits[slot, g, 0], limits[slot, g, 1]
        keeps = [
            (i + half * upper >= begin) & (i + half * upper < end) for i in range(half)
        ]
        p0, p3 = split(orb.at[side, 0, at])
        p1, p2 = split(orb.at[side, 1, at])
        planes = [p0, p1, p2, p3]
        out0, out3 = split(outer_tile)
        down3 = select(half - 1 + half * upper >= begin + depth, out3)
        up0 = select(half * upper < end - depth, out0)
        finish(side, at, planes, swap(p3, down3), swap(up0, p0), keeps)

    @pl.loop(0, groups)
    def _(g):
        edge = split(orb.at[0, 0, groups + g])[1]
        outer_frame(1, groups + g, 1, g, True, edge, raw.at[0, g], raw.at[1, g])
        edge = split(orb.at[1, 0, 2 * groups + g])[0]
        theirs = groups + g
        outer_frame(0, groups + theirs, 2, g, False, edge, raw.at[0, theirs], raw.at[1, theirs])

    for step in steps:
        par, low = mate(step)
        arrive(tile_target(3, par, low), tile_recv.at[3, par * groups + low])

    @pl.loop(0, groups)
    def _(g):
        main_frame(0, groups + g, 1, g, raw.at[0, g])
        main_frame(1, 2 * groups + g, 2, g, raw.at[0, groups + g])

    for side in range(2):
        arrive(halo_in.at[side], halo_recv.at[side])
        for g in range(groups):
            for index in range(2):
                arrive(far.at[side, index, g], far_recv.at[side, index, g])
            edge = split(halo_in.at[side])[g // 2]
            if g % 2 == side:
                edge = [pltpu.roll(x, per, 0) for x in edge]
            slot = 3 * side
            outer_frame(side, g, slot, g, not side, edge, far.at[side, 0, g], far.at[side, 1, g])

    count = 3 * groups
    wide = count * rows_tile
    for side in range(2):
        for t in range(2):
            columns = orb[side, t].reshape(wide, cells)
            images = rest[side, t].reshape(wide, cells)
            full = jnp.concatenate([columns, columns[: 2 * LANES - wide]], 0)
            part = lax.dot_general(
                jnp.concatenate([columns, images], 0),
                full,
                (((1,), (1,)), ((), ())),
                preferred_element_type=f32,
            )
            if t:
                acc[side] += part
            else:
                acc[side] = part

    quarter = lax.rem(lane8, 16) // per
    own_plane = [quarter == upper + 2 * pi for pi in range(2)]

    def gathered(side, at):
        both = []
        for kind in range(2):
            top = (kind * count + at) * rows_tile
            parts = []
            for v in range(2):
                lanes = slice(v * LANES, (v + 1) * LANES)
                value = jnp.where(own_plane[0], acc[side, top : top + 8, lanes], 0.0)
                value += jnp.where(own_plane[1], acc[side, top + 8 : top + 16, lanes], 0.0)
                value += pltpu.roll(value, per, 0)
                value += pltpu.roll(value, LANES - 4, 1)
                value += pltpu.roll(value, LANES - 8, 1)
                parts.append(value)
            both.append(parts)
        return [jnp.where(low_half, both[0][v], both[1][v]) for v in range(2)]

    left = lane8 < LANES // 2
    even = lax.rem(lane8, 16) < 8
    zero = jnp.zeros((8, LANES), f32)
    for slot in (3, 0, 1, 2):
        for g in range(groups):
            v0, v1 = gathered(0, slot * groups + g) if slot < 3 else (zero, zero)
            w0, w1 = gathered(1, slot % 3 * groups + g) if slot else (zero, zero)
            near_cols = jnp.where(left, v0, v0 + w0)
            far_cols = jnp.where(left, v1 + w1, pltpu.roll(w0, LANES // 2, 1))
            if slot == 3:
                near_cols = jnp.where(left, 0.0, w0)
            rows[slot, g] = jnp.where(even, near_cols, pltpu.roll(far_cols, 8, 1))

    for slot in (3, 0):
        to = lax.rem(base + slabs - 1 + slot, slabs)
        for g in range(groups):
            push(
                rows.at[slot, g],
                got_rows.at[1, mine],
                rows_send.at[slot, g],
                rows_recv.at[1, mine],
                (to, g),
            )
    for step in steps:
        par, low = mate(step)
        source, target = rows.at[1 + par, low], got_rows.at[0, mine]
        if step:
            push(source, target, rows_send.at[1, step], rows_recv.at[0, mine], (base + par, low))
        else:
            pltpu.make_async_copy(source, target, rows_recv.at[0, mine]).start()
    for side in range(2):
        for r in range(team):
            arrive(got_rows.at[side, r], rows_recv.at[side, r])
    sums = []
    for side in range(2):
        total = got_rows[side, 0]
        for r in range(1, team):
            total = total + got_rows[side, r]
        sums.append(total)
    total = jnp.dot(
        jnp.concatenate(sums, 1),
        place[...],
        preferred_element_type=f32,
        precision=lax.Precision.HIGHEST,
    ) * (1.0 / comp)
    out_ref[...] = total + jnp.where(low_half, 0.0, 3.0 * pltpu.roll(total, per, 0))
    for copy in unsent:
        copy.wait_send()


def split_kernel(band_ref, margin_ref, ham_ref):
    per, width = margin_ref.shape
    margin_ref[...] = band_ref[:per, :width]
    ham_ref[...] = band_ref[per:, :width]


def local(slabs, groups, potential, coefficients, box_center, box_extent):
    per, box, comp, cells = coefficients.shape
    depth = potential.shape[0]
    team = 2 * groups
    rows_tile = 4 * per
    assert (depth, per, comp, groups) == (8, 4, team, 4)
    vmem = pl.BlockSpec(memory_space=pltpu.VMEM)
    anywhere = pl.BlockSpec(memory_space=pl.ANY)
    bf16, f32 = jnp.bfloat16, jnp.float32
    tiles = lambda *lead: pltpu.VMEM((*lead, rows_tile, cells), bf16)
    dma = pltpu.SemaphoreType.DMA
    band = pl.pallas_call(
        functools.partial(band_kernel, slabs, groups, depth),
        out_shape=jax.ShapeDtypeStruct((2 * per, LANES), f32),
        in_specs=[anywhere] * 6,
        out_specs=vmem,
        scratch_shapes=[
            pltpu.VMEM(potential.shape, bf16),
            pltpu.SMEM(box_center.shape, jnp.int32),
            pltpu.SMEM(box_extent.shape, jnp.int32),
            pltpu.VMEM((comp * rows_tile, comp * rows_tile), bf16),
            pltpu.VMEM((BLOCK, BLOCK), bf16),
            pltpu.VMEM((per, box, comp, cells), bf16),
            tiles(4, comp),
            tiles(2, team),
            tiles(2, 2, groups),
            tiles(2),
            tiles(2),
            tiles(2, 2, 3 * groups),
            tiles(2, 2, 3 * groups),
            pltpu.VMEM((2, 4 * depth, cells), f32),
            pltpu.VMEM((depth, cells), bf16),
            pltpu.VMEM((depth, cells), bf16),
            pltpu.VMEM((4, groups, 2, 8, LANES), jnp.int32),
            pltpu.VMEM((2, 6 * groups * rows_tile, 2 * LANES), f32),
            pltpu.VMEM((2 * LANES, LANES), f32),
            pltpu.VMEM((4, groups, 2 * per, LANES), f32),
            pltpu.VMEM((2, team, 2 * per, LANES), f32),
            dma((6,)),
            dma,
            dma,
            dma((4, team)),
            dma((4, team)),
            dma((2, team)),
            dma((2, 2, groups)),
            dma((2,)),
            dma((2,)),
            dma((4, team)),
            dma((2, team)),
        ],
        compiler_params=pltpu.CompilerParams(collective_id=0, has_side_effects=True),
        name="band",
    )(potential, box_center, box_extent, *matrices(rows_tile), coefficients)
    out = jax.ShapeDtypeStruct((per, 5 * groups * per), f32)
    return pl.pallas_call(
        split_kernel, out_shape=(out, out), in_specs=[vmem], out_specs=(vmem, vmem), name="split"
    )(band)


def solution(mesh):
    return jax.shard_map(
        functools.partial(local, mesh.shape["slab"], mesh.shape["grp"]),
        mesh=mesh,
        in_specs=(P("slab", None, None), P(("slab", "grp"), None, None, None), P(), P()),
        out_specs=(P(("slab", "grp"), None), P(("slab", "grp"), None)),
        check_vma=False,
    )
```

```python
import functools

import jax
import jax.numpy as jnp
import numpy as np
from jax import lax
from jax.experimental import pallas as pl
from jax.experimental.pallas import tpu as pltpu
from jax.sharding import PartitionSpec as P

COMP = 8
CX = 32
CY = 32
BLOCK = 256
LANES = 128
MESH = pl.DeviceIdType.MESH
PAIRS = ((0, 3), (1, 2))
SHORT = (0, 3, 1, 2)


def haar_signs():
    ids = np.arange(COMP)
    common = ids[:, None] & ids[None, :]
    parity = (common % 2 + common // 2 % 2 + common // 4 % 2) % 2
    return (1 - 2 * parity).astype(np.float32)


def matrices(rows):
    haar = np.einsum("kc,mn->kmnc", haar_signs(), np.eye(rows, dtype=np.float32))
    haar = haar.reshape(COMP * rows, rows * COMP)
    lap = np.zeros((BLOCK, BLOCK), np.float32)
    for i in range(BLOCK):
        if i % CY:
            lap[i - 1, i] = lap[i, i - 1] = -0.5
        if i >= CY:
            lap[i - CY, i] = lap[i, i - CY] = -0.5
    return jnp.asarray(haar, jnp.bfloat16), jnp.asarray(lap, jnp.bfloat16)


def band_kernel(
    slabs,
    groups,
    depth,
    pot_hbm,
    center_hbm,
    extent_hbm,
    haar_hbm,
    lap_hbm,
    coef_hbm,
    out_ref,
    pot_ref,
    center_ref,
    extent_ref,
    haar_ref,
    lap_ref,
    coef,
    frames,
    raw,
    far,
    halo_out,
    orb,
    rest,
    pot,
    pot_out,
    pot_in,
    limits,
    acc,
    place,
    rows,
    got_rows,
    load_sem,
    sent_sem,
    pot_recv,
    outer_recv,
    main_recv,
    far_recv,
    rows_recv,
):
    f32, bf16 = jnp.float32, jnp.bfloat16
    slab = lax.axis_index("slab")
    me = lax.axis_index("grp")
    per, box, comp, cells = coef.shape
    half = depth // 2
    team = 2 * groups
    rows_tile = 4 * per
    odd = lax.rem(slab, 2)
    base = slab - odd
    mine = odd * groups + me
    ahead = lax.rem(slab + 2, slabs)
    behind = lax.rem(slab + slabs - 2, slabs)

    def mate(step):
        low, scale, rest_of, bits = 0, 1, me, step
        while scale < groups:
            bit = lax.rem(rest_of, 2)
            rest_of = rest_of // 2
            low = low + scale * (1 - bit if bits % 2 else bit)
            bits //= 2
            scale *= 2
        par = 1 - odd if bits else odd
        return par, low

    steps = [6, 2, 4, 7, 3, 5, 1, 0]

    loads = [
        pltpu.make_async_copy(source, target, load_sem.at[n])
        for n, (source, target) in enumerate(
            (
                (center_hbm, center_ref),
                (extent_hbm, extent_ref),
                (coef_hbm, coef),
                (haar_hbm, haar_ref),
                (pot_hbm, pot_ref),
                (lap_hbm, lap_ref),
            )
        )
    ]
    for copy in loads:
        copy.start()

    barrier = pltpu.get_barrier_semaphore()
    for step in steps:
        if step:
            par, low = mate(step)
            pl.semaphore_signal(
                barrier, inc=1, device_id=(base + par, low), device_id_type=MESH
            )
    for place_at in (ahead, behind):
        pl.semaphore_signal(barrier, inc=1, device_id=(place_at, me), device_id_type=MESH)

    def push(kind, source, target, recv, to):
        copy = pltpu.make_async_remote_copy(
            src_ref=source,
            dst_ref=target,
            send_sem=sent_sem.at[kind],
            recv_sem=recv,
            device_id=to,
            device_id_type=MESH,
        )
        copy.start()

    def arrive(block, sem):
        pltpu.make_async_copy(block, block, sem).wait()

    def iota(shape, dim):
        return lax.broadcasted_iota(jnp.int32, shape, dim)

    def plane_of(row):
        pair = row // 8
        first = jnp.where(pair == 1, 3, jnp.where(pair == 2, 1, jnp.where(pair == 3, 2, 0)))
        return first + half * (lax.rem(row, 8) // per)

    row8 = iota((8, LANES), 0)
    func = lax.rem(row8, per)
    upper = row8 // per

    def spread(values):
        vec = jnp.full((8, LANES), values[0], jnp.int32)
        for f in range(1, per):
            vec = jnp.where(func == f, values[f], vec)
        return vec

    loads[0].wait()
    loads[1].wait()
    first = (slab * groups + me) * per
    extents = [extent_ref[first + f] for f in range(per)]
    starts = [
        center_ref[first + f] - slab * depth - lax.shift_right_logical(extents[f], 1)
        for f in range(per)
    ]
    start_rows, end_rows = spread(starts), spread([s + e for s, e in zip(starts, extents)])

    def build(index, outer, pairs):
        planes, masks = [], []
        for i in pairs:
            for h in range(2):
                for f in range(per):
                    j = i + half * h
                    if outer:
                        p = j + depth - starts[f]
                        p = jnp.where(p < extents[f], p, p - 2 * depth)
                    else:
                        p = j - starts[f]
                    planes.append(coef[f, jnp.clip(p, 0, box - 1)].astype(f32))
            j = i + half * upper
            if outer:
                masks.append((j < end_rows - depth) | (j >= start_rows + depth))
            else:
                masks.append((j >= start_rows) & (j < end_rows))
        stacked = jnp.concatenate(planes, 0).astype(bf16)
        fine = jnp.dot(haar_ref[...], stacked, preferred_element_type=f32)
        keep = jnp.concatenate(masks, 0)
        for k in range(comp):
            for v in range(cells // LANES):
                at = slice(v * LANES, (v + 1) * LANES)
                part = fine[k * rows_tile : (k + 1) * rows_tile, at]
                frames[index, k, :, at] = jnp.where(keep, part, 0.0).astype(bf16)

    def tile_target(index, par, low):
        if index in (0, 3):
            return orb.at[par, index // 3, (1 + par) * groups + low]
        return raw.at[index - 1, par * groups + low]

    def arrive_main(index):
        arrive(frames.at[0], main_recv.at[index])

    def send_tiles(index):
        for step in steps:
            par, low = mate(step)
            source = frames.at[index, par * groups + low]
            target = tile_target(index, odd, me)
            recv = main_recv.at[index // 3] if index in (0, 3) else outer_recv.at[index - 1, mine]
            if step:
                push(0, source, target, recv, (base + par, low))
            else:
                pltpu.make_async_copy(source, target, recv).start()

    urgent = base // 2 // ((slabs + 2) // 4)
    own_first = 1 - lax.rem(urgent + odd, 2)

    def relay(index, place):
        if place < 2:
            par, low = mate(place)
        else:
            own = place - 2 < 2, place - 2 >= 4
            par = odd + (1 - 2 * odd) * (1 - (own[0] * own_first + own[1] * (1 - own_first)))
            first = mate((2, 3, 0, 1, 2, 3)[place - 2])[1]
            second = mate((0, 1, 2, 3, 2, 3)[place - 2])[1]
            low = own_first * first + (1 - own_first) * second
        if place:
            block = tile_target(index, par, low)
            arrive(block, outer_recv.at[index - 1, par * groups + low])
        else:
            block = frames.at[index, mine]
        push(
            1,
            block,
            far.at[1 - par, (index - 1) * groups + low],
            far_recv.at[1 - par],
            (lax.rem(slab + slabs + 4 * par - 2, slabs), me),
        )

    loads[2].wait()
    loads[3].wait()
    build(1, True, PAIRS[0])
    pl.semaphore_wait(barrier, team + 1)
    send_tiles(1)
    relay(1, 0)
    build(2, True, PAIRS[1])
    relay(2, 0)
    build(0, False, PAIRS[0])
    send_tiles(0)
    send_tiles(2)
    relay(1, 1)
    loads[4].wait()
    loads[5].wait()
    theirs = (1 - odd) * groups + me
    own_pot = pot_ref[...].astype(f32).reshape(depth * comp, cells).astype(bf16)
    at_plane, at_column = iota((16, depth * comp), 0), iota((16, depth * comp), 1)
    pick = jnp.where(at_column == at_plane * comp + theirs, 1.0, 0.0).astype(bf16)
    sent = jnp.dot(pick, own_pot, preferred_element_type=f32)
    pot_out[...] = sent[:depth].astype(bf16)
    at_row, at_column = iota((4 * depth, depth * comp), 0), iota((4 * depth, depth * comp), 1)
    pick = jnp.where(at_column == plane_of(at_row) * comp + mine, 1.0, 0.0).astype(bf16)
    pot[odd] = jnp.dot(pick, own_pot, preferred_element_type=f32)

    push(3, pot_out, pot_in, pot_recv, (base + 1 - odd, me))

    build(3, False, PAIRS[1])
    send_tiles(3)
    relay(2, 1)

    for slot in range(4):
        home = lax.rem(base + slabs - 1 + slot, slabs)
        for g in range(groups):
            at = (home * groups + g) * per
            ext = [extent_ref[at + f] for f in range(per)]
            begin = [
                center_ref[at + f] - home * depth - lax.shift_right_logical(ext[f], 1)
                for f in range(per)
            ]
            limits[slot, g, 0] = spread(begin)
            limits[slot, g, 1] = spread([b + e for b, e in zip(begin, ext)])

    at_row, at_column = iota((2 * LANES, LANES), 0), iota((2 * LANES, LANES), 1)
    lane = lax.rem(at_row, LANES)
    slot_of = lane // 64 + 2 * (lax.rem(lane, 8 * 2) // 8)
    member = lax.rem(lane, 64) // 16 * per + lax.rem(lane, 8)
    near = at_row < LANES
    band = jnp.where(near, slot_of + 1 - odd, slot_of - 1 + 3 * odd)
    fits = (lax.rem(lane, 8) < per) & (band >= 0) & (band < 5)
    fits = fits & (at_column == band * groups * per + member)
    place[...] = jnp.where(fits, 1.0, 0.0)

    low_half = row8 < per
    lane8 = iota((8, LANES), 1)
    vregs = cells // LANES
    blocks = cells // BLOCK
    per_block = BLOCK // LANES

    def split(ref):
        wide = ref[...].astype(f32)
        cut = lambda part: [part[:, v * LANES : (v + 1) * LANES] for v in range(vregs)]
        return cut(wide[:8]), cut(wide[8:])

    for turn in range(2, 8):
        relay(1, turn)
    arrive_main(0)
    for side in range(2):
        edges = [split(orb.at[side, 0, (1 + side) * groups + g])[side] for g in range(groups)]
        for n in range(groups // 2):
            one, two = edges[2 * n], edges[2 * n + 1]
            for v in range(vregs):
                if side:
                    both = jnp.where(low_half, pltpu.roll(one[v], per, 0), two[v])
                else:
                    both = jnp.where(low_half, one[v], pltpu.roll(two[v], per, 0))
                halo_out[side, 8 * n : 8 * n + 8, v * LANES : (v + 1) * LANES] = both.astype(bf16)
        push(
            2,
            halo_out.at[side],
            far.at[1 - side, 2 * groups],
            far_recv.at[1 - side],
            (ahead if side else behind, me),
        )
    for turn in range(2, 8):
        relay(2, turn)
    for index in (1, 2):
        arrive(tile_target(index, odd, me), outer_recv.at[index - 1, mine])
    arrive(pot_in, pot_recv)
    padded = jnp.concatenate([pot_in[...].astype(f32), jnp.zeros((depth, cells), f32)], 0)
    at_row, at_column = iota((4 * depth, 2 * depth), 0), iota((4 * depth, 2 * depth), 1)
    pick = jnp.where(at_column == plane_of(at_row), 1.0, 0.0).astype(bf16)
    pot[1 - odd] = jnp.dot(pick, padded.astype(bf16), preferred_element_type=f32)

    def swap(low_rows, high_rows):
        return [
            pltpu.roll(jnp.where(low_half, a, b), per, 0) for a, b in zip(low_rows, high_rows)
        ]

    def select(keep, rows_in):
        return [jnp.where(keep, x, 0.0) for x in rows_in]

    def finish(side, at, planes, before, after, keeps):
        tiles = [orb.at[side, t, at] for t in range(2)]
        stack = []
        for q in range(blocks):
            for t in range(2):
                stack.append(tiles[t][:, q * BLOCK : (q + 1) * BLOCK])
        beside = jnp.dot(jnp.concatenate(stack, 0), lap_ref[...], preferred_element_type=f32)
        shifted = [before, *planes, after]
        for v in range(vregs):
            done = {}
            q, part = divmod(v, per_block)
            for n, i in enumerate(SHORT):
                total = shifted[i][v] + shifted[i + 2][v]
                if part == 0 and v:
                    moved = pltpu.roll(planes[i][v - 1], CY, 1)
                    total = total + jnp.where(lane8 < CY, moved, 0.0)
                if part == per_block - 1 and v < vregs - 1:
                    moved = pltpu.roll(planes[i][v + 1], LANES - CY, 1)
                    total = total + jnp.where(lane8 >= LANES - CY, moved, 0.0)
                top = (q * 4 + n) * 8
                value = beside[top : top + 8, part * LANES : (part + 1) * LANES]
                value = value - 0.5 * total
                value = value + pot[side, n * 8 : n * 8 + 8, v * LANES : (v + 1) * LANES] * (
                    planes[i][v]
                )
                done[i] = jnp.where(keeps[i], value, 0.0)
            for t in range(2):
                both = jnp.concatenate([done[i] for i in PAIRS[t]], 0)
                rest[side, t, at, :, v * LANES : (v + 1) * LANES] = both.astype(bf16)

    def outer_frame(side, at, slot, g, up, edge, first_tile, second_tile):
        begin, end = limits[slot, g, 0], limits[slot, g, 1]
        if up:
            keeps = [i + half * upper < end - depth for i in range(half)]
        else:
            keeps = [i + half * upper >= begin + depth for i in range(half)]
        p0, p3 = split(first_tile)
        p1, p2 = split(second_tile)
        planes = [select(keeps[i], p) for i, p in enumerate((p0, p1, p2, p3))]
        for v in range(vregs):
            for t in range(2):
                both = jnp.concatenate([planes[i][v] for i in PAIRS[t]], 0)
                orb[side, t, at, :, v * LANES : (v + 1) * LANES] = both.astype(bf16)
        zero = [jnp.zeros((8, LANES), f32)] * vregs
        if up:
            before, after = swap(planes[3], edge), swap(zero, planes[0])
        else:
            before, after = swap(planes[3], zero), swap(edge, planes[0])
        finish(side, at, planes, before, after, keeps)

    def main_frame(side, at, slot, g, outer_tile):
        begin, end = limits[slot, g, 0], limits[slot, g, 1]
        keeps = [
            (i + half * upper >= begin) & (i + half * upper < end) for i in range(half)
        ]
        p0, p3 = split(orb.at[side, 0, at])
        p1, p2 = split(orb.at[side, 1, at])
        planes = [p0, p1, p2, p3]
        out0, out3 = split(outer_tile)
        down3 = select(half - 1 + half * upper >= begin + depth, out3)
        up0 = select(half * upper < end - depth, out0)
        finish(side, at, planes, swap(p3, down3), swap(up0, p0), keeps)

    @pl.loop(0, groups)
    def _(g):
        edge = split(orb.at[0, 0, groups + g])[1]
        outer_frame(1, groups + g, 1, g, True, edge, raw.at[0, g], raw.at[1, g])
        edge = split(orb.at[1, 0, 2 * groups + g])[0]
        theirs = groups + g
        outer_frame(0, groups + theirs, 2, g, False, edge, raw.at[0, theirs], raw.at[1, theirs])

    quarter = lax.rem(lane8, 16) // per
    own_plane = [quarter == upper + 2 * pi for pi in range(2)]

    def gathered(side, at):
        both = []
        for kind in range(2):
            top = (kind * count + at) * rows_tile
            parts = []
            for v in range(2):
                lanes = slice(v * LANES, (v + 1) * LANES)
                value = jnp.where(own_plane[0], acc[side, top : top + 8, lanes], 0.0)
                value += jnp.where(own_plane[1], acc[side, top + 8 : top + 16, lanes], 0.0)
                value += pltpu.roll(value, per, 0)
                value += pltpu.roll(value, LANES - 4, 1)
                value += pltpu.roll(value, LANES - 8, 1)
                parts.append(value)
            both.append(parts)
        return [jnp.where(low_half, both[0][v], both[1][v]) for v in range(2)]

    left = lane8 < LANES // 2
    even = lax.rem(lane8, 16) < 8
    count = 3 * groups
    wide = count * rows_tile

    def far_side(side):
        arrive(far.at[side], far_recv.at[side])
        for g in range(groups):
            edge = split(far.at[side, 2 * groups])[g // 2]
            if g % 2 == side:
                edge = [pltpu.roll(x, per, 0) for x in edge]
            outer_frame(side, g, 3 * side, g, not side, edge, far.at[side, g], far.at[side, groups + g])

    def products(side):
        for t in range(2):
            columns = orb[side, t].reshape(wide, cells)
            images = rest[side, t].reshape(wide, cells)
            full = jnp.concatenate([columns, columns[: 2 * LANES - wide]], 0)
            part = lax.dot_general(
                jnp.concatenate([columns, images], 0),
                full,
                (((1,), (1,)), ((), ())),
                preferred_element_type=f32,
            )
            if t:
                acc[side] += part
            else:
                acc[side] = part
        for g in range(groups):
            one, two = gathered(side, g)
            if side:
                near_cols = jnp.where(left, 0.0, one)
                far_cols = jnp.where(left, two, pltpu.roll(one, LANES // 2, 1))
            else:
                near_cols, far_cols = one, jnp.where(left, two, 0.0)
            rows[3 * side, g] = jnp.where(even, near_cols, pltpu.roll(far_cols, 8, 1))

    arrive_main(1)
    @pl.loop(0, groups)
    def _(g):
        main_frame(0, groups + g, 1, g, raw.at[0, g])
        main_frame(1, 2 * groups + g, 2, g, raw.at[0, groups + g])
    for turn in range(2):
        now = urgent + turn - 2 * urgent * turn
        for side in range(2):
            pl.when(now == side)(functools.partial(far_side, side))
        for side in range(2):
            pl.when(now == side)(functools.partial(products, side))
        for g in range(groups):
            push(
                4,
                rows.at[3 * now, g],
                got_rows.at[team + mine],
                rows_recv,
                (lax.rem(base + slabs - 1 + 3 * now, slabs), g),
            )
    for slot in (1, 2):
        for g in range(groups):
            v0, v1 = gathered(0, slot * groups + g)
            w0, w1 = gathered(1, slot * groups + g)
            near_cols = jnp.where(left, v0, v0 + w0)
            far_cols = jnp.where(left, v1 + w1, pltpu.roll(w0, LANES // 2, 1))
            rows[slot, g] = jnp.where(even, near_cols, pltpu.roll(far_cols, 8, 1))
    for step in steps:
        par, low = mate(step)
        source, target = rows.at[1 + par, low], got_rows.at[mine]
        if step:
            push(4, source, target, rows_recv, (base + par, low))
        else:
            pltpu.make_async_copy(source, target, rows_recv).start()
    arrive(got_rows, rows_recv)
    sums = []
    for side in range(2):
        total = got_rows[side * team]
        for r in range(1, team):
            total = total + got_rows[side * team + r]
        sums.append(total)
    total = jnp.dot(
        jnp.concatenate(sums, 1),
        place[...],
        preferred_element_type=f32,
        precision=lax.Precision.HIGHEST,
    ) * (1.0 / comp)
    out_ref[...] = total + jnp.where(low_half, 0.0, 3.0 * pltpu.roll(total, per, 0))
    for kind, block in enumerate(
        (frames.at[:, : comp - 1], raw, halo_out, pot_out, got_rows.at[: 2 * team - 1])
    ):
        arrive(block, sent_sem.at[kind])


def split_kernel(band_ref, margin_ref, ham_ref):
    per, width = margin_ref.shape
    margin_ref[...] = band_ref[:per, :width]
    ham_ref[...] = band_ref[per:, :width]


def local(slabs, groups, potential, coefficients, box_center, box_extent):
    per, box, comp, cells = coefficients.shape
    depth = potential.shape[0]
    team = 2 * groups
    rows_tile = 4 * per
    assert (depth, per, comp, groups) == (8, 4, team, 4)
    vmem = pl.BlockSpec(memory_space=pltpu.VMEM)
    anywhere = pl.BlockSpec(memory_space=pl.ANY)
    bf16, f32 = jnp.bfloat16, jnp.float32
    tiles = lambda *lead: pltpu.VMEM((*lead, rows_tile, cells), bf16)
    dma = pltpu.SemaphoreType.DMA
    band = pl.pallas_call(
        functools.partial(band_kernel, slabs, groups, depth),
        out_shape=jax.ShapeDtypeStruct((2 * per, LANES), f32),
        in_specs=[anywhere] * 6,
        out_specs=vmem,
        scratch_shapes=[
            pltpu.VMEM(potential.shape, bf16),
            pltpu.SMEM(box_center.shape, jnp.int32),
            pltpu.SMEM(box_extent.shape, jnp.int32),
            pltpu.VMEM((comp * rows_tile, comp * rows_tile), bf16),
            pltpu.VMEM((BLOCK, BLOCK), bf16),
            pltpu.VMEM((per, box, comp, cells), bf16),
            tiles(4, comp),
            tiles(2, team),
            tiles(2, 2 * groups + 1),
            tiles(2),
            tiles(2, 2, 3 * groups),
            tiles(2, 2, 3 * groups),
            pltpu.VMEM((2, 4 * depth, cells), f32),
            pltpu.VMEM((depth, cells), bf16),
            pltpu.VMEM((depth, cells), bf16),
            pltpu.VMEM((4, groups, 2, 8, LANES), jnp.int32),
            pltpu.VMEM((2, 6 * groups * rows_tile, 2 * LANES), f32),
            pltpu.VMEM((2 * LANES, LANES), f32),
            pltpu.VMEM((4, groups, 2 * per, LANES), f32),
            pltpu.VMEM((2 * team, 2 * per, LANES), f32),
            dma((6,)),
            dma((5,)),
            dma,
            dma((2, team)),
            dma((2,)),
            dma((2,)),
            dma,
        ],
        compiler_params=pltpu.CompilerParams(collective_id=0, has_side_effects=True),
        name="band",
    )(potential, box_center, box_extent, *matrices(rows_tile), coefficients)
    out = jax.ShapeDtypeStruct((per, 5 * groups * per), f32)
    return pl.pallas_call(
        split_kernel, out_shape=(out, out), in_specs=[vmem], out_specs=(vmem, vmem), name="split"
    )(band)


def solution(mesh):
    return jax.shard_map(
        functools.partial(local, mesh.shape["slab"], mesh.shape["grp"]),
        mesh=mesh,
        in_specs=(P("slab", None, None), P(("slab", "grp"), None, None, None), P(), P()),
        out_specs=(P(("slab", "grp"), None), P(("slab", "grp"), None)),
        check_vma=False,
    )
```

```python
import functools

import jax
import jax.numpy as jnp
import numpy as np
from jax import lax
from jax.experimental import pallas as pl
from jax.experimental.pallas import tpu as pltpu
from jax.sharding import PartitionSpec as P

COMP = 8
CX = 32
CY = 32
BLOCK = 256
LANES = 128
MESH = pl.DeviceIdType.MESH
PAIRS = ((0, 3), (1, 2))
SHORT = (0, 3, 1, 2)


def haar_signs():
    ids = np.arange(COMP)
    common = ids[:, None] & ids[None, :]
    parity = (common % 2 + common // 2 % 2 + common // 4 % 2) % 2
    return (1 - 2 * parity).astype(np.float32)


def matrices(rows):
    haar = np.einsum("kc,mn->kmnc", haar_signs(), np.eye(rows, dtype=np.float32))
    haar = haar.reshape(COMP * rows, rows * COMP)
    lap = np.zeros((BLOCK, BLOCK), np.float32)
    for i in range(BLOCK):
        if i % CY:
            lap[i - 1, i] = lap[i, i - 1] = -0.5
        if i >= CY:
            lap[i - CY, i] = lap[i, i - CY] = -0.5
    return jnp.asarray(haar, jnp.bfloat16), jnp.asarray(lap, jnp.bfloat16)


def band_kernel(
    slabs,
    groups,
    depth,
    pot_hbm,
    center_hbm,
    extent_hbm,
    haar_hbm,
    lap_hbm,
    coef_hbm,
    out_ref,
    pot_ref,
    center_ref,
    extent_ref,
    haar_ref,
    lap_ref,
    coef,
    frames,
    raw,
    far,
    orb,
    rest,
    pot,
    pot_out,
    pot_in,
    limits,
    acc,
    place,
    rows,
    got_rows,
    load_sem,
    sent_sem,
    pot_recv,
    outer_recv,
    main_recv,
    far_recv,
    rows_recv,
):
    f32, bf16 = jnp.float32, jnp.bfloat16
    slab = lax.axis_index("slab")
    me = lax.axis_index("grp")
    per, box, comp, cells = coef.shape
    half = depth // 2
    team = 2 * groups
    rows_tile = 4 * per
    odd = lax.rem(slab, 2)
    base = slab - odd
    mine = odd * groups + me
    ahead = lax.rem(slab + 2, slabs)
    behind = lax.rem(slab + slabs - 2, slabs)

    def mate(step):
        low, scale, rest_of, bits = 0, 1, me, step
        while scale < groups:
            bit = lax.rem(rest_of, 2)
            rest_of = rest_of // 2
            low = low + scale * (1 - bit if bits % 2 else bit)
            bits //= 2
            scale *= 2
        par = 1 - odd if bits else odd
        return par, low

    steps = [6, 2, 4, 7, 3, 5, 1, 0]

    loads = [
        pltpu.make_async_copy(source, target, load_sem.at[n])
        for n, (source, target) in enumerate(
            (
                (center_hbm, center_ref),
                (extent_hbm, extent_ref),
                (coef_hbm, coef),
                (haar_hbm, haar_ref),
                (pot_hbm, pot_ref),
                (lap_hbm, lap_ref),
            )
        )
    ]
    for copy in loads:
        copy.start()

    barrier = pltpu.get_barrier_semaphore()
    for step in steps:
        if step:
            par, low = mate(step)
            pl.semaphore_signal(
                barrier, inc=1, device_id=(base + par, low), device_id_type=MESH
            )
    for place_at in (ahead, behind):
        pl.semaphore_signal(barrier, inc=1, device_id=(place_at, me), device_id_type=MESH)

    def push(kind, source, target, recv, to):
        copy = pltpu.make_async_remote_copy(
            src_ref=source,
            dst_ref=target,
            send_sem=sent_sem.at[kind],
            recv_sem=recv,
            device_id=to,
            device_id_type=MESH,
        )
        copy.start()

    def arrive(block, sem):
        pltpu.make_async_copy(block, block, sem).wait()

    def iota(shape, dim):
        return lax.broadcasted_iota(jnp.int32, shape, dim)

    def plane_of(row):
        pair = row // 8
        first = jnp.where(pair == 1, 3, jnp.where(pair == 2, 1, jnp.where(pair == 3, 2, 0)))
        return first + half * (lax.rem(row, 8) // per)

    row8 = iota((8, LANES), 0)
    func = lax.rem(row8, per)
    upper = row8 // per

    def spread(values):
        vec = jnp.full((8, LANES), values[0], jnp.int32)
        for f in range(1, per):
            vec = jnp.where(func == f, values[f], vec)
        return vec

    loads[0].wait()
    loads[1].wait()
    first = (slab * groups + me) * per
    extents = [extent_ref[first + f] for f in range(per)]
    starts = [
        center_ref[first + f] - slab * depth - lax.shift_right_logical(extents[f], 1)
        for f in range(per)
    ]
    start_rows, end_rows = spread(starts), spread([s + e for s, e in zip(starts, extents)])

    def build(index, outer, pairs):
        planes, masks = [], []
        for i in pairs:
            for h in range(2):
                for f in range(per):
                    j = i + half * h
                    away = j + depth - starts[f]
                    away = jnp.where(away < extents[f], away, away - 2 * depth)
                    near = j - starts[f]
                    if j == depth - 1:
                        p = odd * (near if outer else away)
                        p += (1 - odd) * (away if outer else near)
                    else:
                        p = away if outer else near
                    planes.append(coef[f, jnp.clip(p, 0, box - 1)].astype(f32))
            j = i + half * upper
            away = (j < end_rows - depth) | (j >= start_rows + depth)
            near = (j >= start_rows) & (j < end_rows)
            traded = (j == depth - 1) & (odd == 1)
            masks.append(jnp.where(traded != outer, away.astype(jnp.int32), near.astype(jnp.int32)) == 1)
        stacked = jnp.concatenate(planes, 0).astype(bf16)
        fine = jnp.dot(haar_ref[...], stacked, preferred_element_type=f32)
        keep = jnp.concatenate(masks, 0)
        for k in range(comp):
            for v in range(cells // LANES):
                at = slice(v * LANES, (v + 1) * LANES)
                part = fine[k * rows_tile : (k + 1) * rows_tile, at]
                frames[index, k, :, at] = jnp.where(keep, part, 0.0).astype(bf16)

    def tile_target(index, par, low):
        if index in (0, 3):
            return orb.at[par, index // 3, (1 + par) * groups + low]
        return raw.at[index - 1, par * groups + low]

    def arrive_main(index):
        arrive(frames.at[0], main_recv.at[index])

    def send_tiles(index):
        for step in steps:
            par, low = mate(step)
            source = frames.at[index, par * groups + low]
            target = tile_target(index, odd, me)
            if index in (0, 3):
                recv = main_recv.at[index // 3]
            else:
                recv = outer_recv.at[index - 1, mine]
            if step:
                push(0, source, target, recv, (base + par, low))
            else:
                pltpu.make_async_copy(source, target, recv).start()

    urgent = base // 2 // ((slabs + 2) // 4)
    own_first = 1 - lax.rem(urgent + odd, 2)

    row_wide = iota((8, cells), 0)

    def relay(index, place):
        if place < 2:
            par, low = mate(place)
        else:
            own = place - 2 < 2, place - 2 >= 4
            par = odd + (1 - 2 * odd) * (1 - (own[0] * own_first + own[1] * (1 - own_first)))
            first = mate((2, 3, 0, 1, 2, 3)[place - 2])[1]
            second = mate((0, 1, 2, 3, 2, 3)[place - 2])[1]
            low = own_first * first + (1 - own_first) * second
        if place:
            block = tile_target(index, par, low)
            arrive(block, outer_recv.at[index - 1, par * groups + low])
        else:
            block = frames.at[index, mine]
        push(
            1,
            block,
            far.at[1 - par, (index - 1) * groups + low],
            far_recv.at[1 - par],
            (lax.rem(slab + slabs + 4 * par - 2, slabs), me),
        )

    loads[2].wait()
    loads[3].wait()
    build(1, True, PAIRS[1])
    pl.semaphore_wait(barrier, team + 1)
    send_tiles(1)
    relay(1, 0)
    build(2, True, PAIRS[0])
    relay(2, 0)
    send_tiles(2)
    relay(1, 1)
    build(0, False, PAIRS[0])
    send_tiles(0)
    loads[4].wait()
    loads[5].wait()
    theirs = (1 - odd) * groups + me
    own_pot = pot_ref[...].astype(f32).reshape(depth * comp, cells).astype(bf16)
    at_plane, at_column = iota((16, depth * comp), 0), iota((16, depth * comp), 1)
    pick = jnp.where(at_column == at_plane * comp + theirs, 1.0, 0.0).astype(bf16)
    sent = jnp.dot(pick, own_pot, preferred_element_type=f32)
    pot_out[...] = sent[:depth].astype(bf16)
    at_row, at_column = iota((4 * depth, depth * comp), 0), iota((4 * depth, depth * comp), 1)
    pick = jnp.where(at_column == plane_of(at_row) * comp + mine, 1.0, 0.0).astype(bf16)
    pot[odd] = jnp.dot(pick, own_pot, preferred_element_type=f32)

    push(2, pot_out, pot_in, pot_recv, (base + 1 - odd, me))

    build(3, False, PAIRS[1])
    send_tiles(3)
    relay(2, 1)

    for slot in range(4):
        home = lax.rem(base + slabs - 1 + slot, slabs)
        for g in range(groups):
            at = (home * groups + g) * per
            ext = [extent_ref[at + f] for f in range(per)]
            begin = [
                center_ref[at + f] - home * depth - lax.shift_right_logical(ext[f], 1)
                for f in range(per)
            ]
            limits[slot, g, 0] = spread(begin)
            limits[slot, g, 1] = spread([b + e for b, e in zip(begin, ext)])

    at_row, at_column = iota((2 * LANES, LANES), 0), iota((2 * LANES, LANES), 1)
    lane = lax.rem(at_row, LANES)
    slot_of = lane // 64 + 2 * (lax.rem(lane, 8 * 2) // 8)
    member = lax.rem(lane, 64) // 16 * per + lax.rem(lane, 8)
    near = at_row < LANES
    band = jnp.where(near, slot_of + 1 - odd, slot_of - 1 + 3 * odd)
    fits = (lax.rem(lane, 8) < per) & (band >= 0) & (band < 5)
    fits = fits & (at_column == band * groups * per + member)
    place[...] = jnp.where(fits, 1.0, 0.0)

    low_half = row8 < per
    lane8 = iota((8, LANES), 1)
    vregs = cells // LANES
    blocks = cells // BLOCK
    per_block = BLOCK // LANES

    def split(ref):
        wide = ref[...].astype(f32)
        cut = lambda part: [part[:, v * LANES : (v + 1) * LANES] for v in range(vregs)]
        return cut(wide[:8]), cut(wide[8:])

    for turn in range(2, 8):
        relay(1, turn)
    for turn in range(2, 8):
        relay(2, turn)
    arrive_main(0)
    for index in (1, 2):
        arrive(tile_target(index, odd, me), outer_recv.at[index - 1, mine])
    arrive(pot_in, pot_recv)
    padded = jnp.concatenate([pot_in[...].astype(f32), jnp.zeros((depth, cells), f32)], 0)
    at_row, at_column = iota((4 * depth, 2 * depth), 0), iota((4 * depth, 2 * depth), 1)
    pick = jnp.where(at_column == plane_of(at_row), 1.0, 0.0).astype(bf16)
    pot[1 - odd] = jnp.dot(pick, padded.astype(bf16), preferred_element_type=f32)

    def swap(low_rows, high_rows):
        return [
            pltpu.roll(jnp.where(low_half, a, b), per, 0) for a, b in zip(low_rows, high_rows)
        ]

    def select(keep, rows_in):
        return [jnp.where(keep, x, 0.0) for x in rows_in]

    def finish(side, at, planes, before, after, keeps):
        tiles = [orb.at[side, t, at] for t in range(2)]
        stack = []
        for q in range(blocks):
            for t in range(2):
                stack.append(tiles[t][:, q * BLOCK : (q + 1) * BLOCK])
        beside = jnp.dot(jnp.concatenate(stack, 0), lap_ref[...], preferred_element_type=f32)
        shifted = [before, *planes, after]
        for v in range(vregs):
            done = {}
            q, part = divmod(v, per_block)
            for n, i in enumerate(SHORT):
                total = shifted[i][v] + shifted[i + 2][v]
                if part == 0 and v:
                    moved = pltpu.roll(planes[i][v - 1], CY, 1)
                    total = total + jnp.where(lane8 < CY, moved, 0.0)
                if part == per_block - 1 and v < vregs - 1:
                    moved = pltpu.roll(planes[i][v + 1], LANES - CY, 1)
                    total = total + jnp.where(lane8 >= LANES - CY, moved, 0.0)
                top = (q * 4 + n) * 8
                value = beside[top : top + 8, part * LANES : (part + 1) * LANES]
                value = value - 0.5 * total
                value = value + pot[side, n * 8 : n * 8 + 8, v * LANES : (v + 1) * LANES] * (
                    planes[i][v]
                )
                done[i] = jnp.where(keeps[i], value, 0.0)
            for t in range(2):
                both = jnp.concatenate([done[i] for i in PAIRS[t]], 0)
                rest[side, t, at, :, v * LANES : (v + 1) * LANES] = both.astype(bf16)

    def outer_frame(side, at, slot, g, up, edge, first, second_tile):
        begin, end = limits[slot, g, 0], limits[slot, g, 1]
        if up:
            keeps = [i + half * upper < end - depth for i in range(half)]
        else:
            keeps = [i + half * upper >= begin + depth for i in range(half)]
        p0, p3 = first
        p1, p2 = split(second_tile)
        planes = [select(keeps[i], p) for i, p in enumerate((p0, p1, p2, p3))]
        for v in range(vregs):
            for t in range(2):
                both = jnp.concatenate([planes[i][v] for i in PAIRS[t]], 0)
                orb[side, t, at, :, v * LANES : (v + 1) * LANES] = both.astype(bf16)
        zero = [jnp.zeros((8, LANES), f32)] * vregs
        if up:
            before, after = swap(planes[3], edge), swap(zero, planes[0])
        else:
            before, after = swap(planes[3], zero), swap(edge or zero, planes[0])
        finish(side, at, planes, before, after, keeps)

    def main_frame(side, at, slot, g, up_tile, down_tile):
        begin, end = limits[slot, g, 0], limits[slot, g, 1]
        keeps = [
            (i + half * upper >= begin) & (i + half * upper < end) for i in range(half)
        ]
        p0, p3 = split(orb.at[side, 0, at])
        p1, p2 = split(orb.at[side, 1, at])
        planes = [p0, p1, p2, p3]
        out0, out3 = split(up_tile)[0], split(down_tile)[1]
        down3 = select(half - 1 + half * upper >= begin + depth, out3)
        up0 = select(half * upper < end - depth, out0)
        finish(side, at, planes, swap(p3, down3), swap(up0, p0), keeps)

    @pl.loop(0, groups)
    def _(g):
        edge = split(orb.at[0, 0, groups + g])[1]
        outer_frame(1, groups + g, 1, g, True, edge, split(raw.at[1, g]), raw.at[0, g])
        theirs = groups + g
        main0, main3 = split(orb.at[1, 0, groups + theirs])
        out0, out3 = split(raw.at[1, theirs])
        for v in range(vregs):
            both = jnp.concatenate([main0[v], jnp.where(low_half, main3[v], out3[v])], 0)
            orb[1, 0, groups + theirs, :, v * LANES : (v + 1) * LANES] = both.astype(bf16)
        out3 = [jnp.where(low_half, a, b) for a, b in zip(out3, main3)]
        outer_frame(0, groups + theirs, 2, g, False, main0, (out0, out3), raw.at[0, theirs])

    quarter = lax.rem(lane8, 16) // per
    own_plane = [quarter == upper + 2 * pi for pi in range(2)]

    def gathered(side, at):
        both = []
        for kind in range(2):
            top = (kind * count + at) * rows_tile
            parts = []
            for v in range(2):
                lanes = slice(v * LANES, (v + 1) * LANES)
                value = jnp.where(own_plane[0], acc[side, top : top + 8, lanes], 0.0)
                value += jnp.where(own_plane[1], acc[side, top + 8 : top + 16, lanes], 0.0)
                value += pltpu.roll(value, per, 0)
                value += pltpu.roll(value, LANES - 4, 1)
                value += pltpu.roll(value, LANES - 8, 1)
                parts.append(value)
            both.append(parts)
        return [jnp.where(low_half, both[0][v], both[1][v]) for v in range(2)]

    left = lane8 < LANES // 2
    even = lax.rem(lane8, 16) < 8
    count = 3 * groups
    wide = count * rows_tile

    def limits_wide(slot, g):
        return jnp.concatenate([limits[slot, g, 0]] * vregs, 1)

    def far_side(side):
        arrive(far.at[side], far_recv.at[side])
        for g in range(groups):
            edge = None if side else split(far.at[0, groups + g])[1]
            first, second = split(far.at[side, groups + g]), far.at[side, g]
            outer_frame(side, g, 3 * side, g, not side, edge, first, second)

    def products(side):
        for t in range(2):
            columns = orb[side, t].reshape(wide, cells)
            images = rest[side, t].reshape(wide, cells)
            full = jnp.concatenate([columns, columns[: 2 * LANES - wide]], 0)
            part = lax.dot_general(
                jnp.concatenate([columns, images], 0),
                full,
                (((1,), (1,)), ((), ())),
                preferred_element_type=f32,
            )
            if t:
                acc[side] += part
            else:
                acc[side] = part
        if side == 0:
            tops = []
            for g in range(groups):
                plane0 = pltpu.roll(orb[0, 0, groups + g][:8].astype(f32), per, 0)
                here = (row_wide >= per) & (limits_wide(1, g) < 0)
                plane0 = jnp.where(here, -0.5 * plane0, 0.0)
                tops += [jnp.zeros((8, cells), f32), plane0]
            others = [far[0, groups + g] for g in range(groups)] + [raw[1, g] for g in range(groups)]
            top = (count + groups) * rows_tile
            acc[0, top : top + groups * rows_tile, :LANES] += lax.dot_general(
                jnp.concatenate(tops, 0).astype(bf16),
                jnp.concatenate(others, 0),
                (((1,), (1,)), ((), ())),
                preferred_element_type=f32,
            )
        for g in range(groups):
            one, two = gathered(side, g)
            if side:
                near_cols = jnp.where(left, 0.0, one)
                far_cols = jnp.where(left, two, pltpu.roll(one, LANES // 2, 1))
            else:
                near_cols, far_cols = one, jnp.where(left, two, 0.0)
            rows[3 * side, g] = jnp.where(even, near_cols, pltpu.roll(far_cols, 8, 1))

    arrive_main(1)
    @pl.loop(0, groups)
    def _(g):
        main_frame(0, groups + g, 1, g, raw.at[1, g], raw.at[1, g])
        own = 2 * groups + g
        main_frame(1, own, 2, g, raw.at[1, groups + g], orb.at[0, 0, own])
    for turn in range(2):
        now = urgent + turn - 2 * urgent * turn
        for side in range(2):
            pl.when(now == side)(functools.partial(far_side, side))
        for side in range(2):
            pl.when(now == side)(functools.partial(products, side))
        for g in range(groups):
            push(
                3,
                rows.at[3 * now, g],
                got_rows.at[team + mine],
                rows_recv,
                (lax.rem(base + slabs - 1 + 3 * now, slabs), g),
            )
    for slot in (1, 2):
        for g in range(groups):
            v0, v1 = gathered(0, slot * groups + g)
            w0, w1 = gathered(1, slot * groups + g)
            near_cols = jnp.where(left, v0, v0 + w0)
            far_cols = jnp.where(left, v1 + w1, pltpu.roll(w0, LANES // 2, 1))
            rows[slot, g] = jnp.where(even, near_cols, pltpu.roll(far_cols, 8, 1))
    for step in steps:
        par, low = mate(step)
        source, target = rows.at[1 + par, low], got_rows.at[mine]
        if step:
            push(3, source, target, rows_recv, (base + par, low))
        else:
            pltpu.make_async_copy(source, target, rows_recv).start()
    arrive(got_rows, rows_recv)
    sums = []
    for side in range(2):
        total = got_rows[side * team]
        for r in range(1, team):
            total = total + got_rows[side * team + r]
        sums.append(total)
    total = jnp.dot(
        jnp.concatenate(sums, 1),
        place[...],
        preferred_element_type=f32,
        precision=lax.Precision.HIGHEST,
    ) * (1.0 / comp)
    out_ref[...] = total + jnp.where(low_half, 0.0, 3.0 * pltpu.roll(total, per, 0))
    for kind, block in enumerate(
        (frames.at[:, : comp - 1], raw, pot_out, got_rows.at[: 2 * team - 1])
    ):
        arrive(block, sent_sem.at[kind])


def split_kernel(band_ref, margin_ref, ham_ref):
    per, width = margin_ref.shape
    margin_ref[...] = band_ref[:per, :width]
    ham_ref[...] = band_ref[per:, :width]


def local(slabs, groups, potential, coefficients, box_center, box_extent):
    per, box, comp, cells = coefficients.shape
    depth = potential.shape[0]
    team = 2 * groups
    rows_tile = 4 * per
    assert (depth, per, comp, groups) == (8, 4, team, 4)
    vmem = pl.BlockSpec(memory_space=pltpu.VMEM)
    anywhere = pl.BlockSpec(memory_space=pl.ANY)
    bf16, f32 = jnp.bfloat16, jnp.float32
    tiles = lambda *lead: pltpu.VMEM((*lead, rows_tile, cells), bf16)
    dma = pltpu.SemaphoreType.DMA
    band = pl.pallas_call(
        functools.partial(band_kernel, slabs, groups, depth),
        out_shape=jax.ShapeDtypeStruct((2 * per, LANES), f32),
        in_specs=[anywhere] * 6,
        out_specs=vmem,
        scratch_shapes=[
            pltpu.VMEM(potential.shape, bf16),
            pltpu.SMEM(box_center.shape, jnp.int32),
            pltpu.SMEM(box_extent.shape, jnp.int32),
            pltpu.VMEM((comp * rows_tile, comp * rows_tile), bf16),
            pltpu.VMEM((BLOCK, BLOCK), bf16),
            pltpu.VMEM((per, box, comp, cells), bf16),
            tiles(4, comp),
            tiles(2, team),
            tiles(2, 2 * groups),
            tiles(2, 2, 3 * groups),
            tiles(2, 2, 3 * groups),
            pltpu.VMEM((2, 4 * depth, cells), f32),
            pltpu.VMEM((depth, cells), bf16),
            pltpu.VMEM((depth, cells), bf16),
            pltpu.VMEM((4, groups, 2, 8, LANES), jnp.int32),
            pltpu.VMEM((2, 6 * groups * rows_tile, 2 * LANES), f32),
            pltpu.VMEM((2 * LANES, LANES), f32),
            pltpu.VMEM((4, groups, 2 * per, LANES), f32),
            pltpu.VMEM((2 * team, 2 * per, LANES), f32),
            dma((6,)),
            dma((4,)),
            dma,
            dma((2, team)),
            dma((2,)),
            dma((2,)),
            dma,
        ],
        compiler_params=pltpu.CompilerParams(collective_id=0, has_side_effects=True),
        name="band",
    )(potential, box_center, box_extent, *matrices(rows_tile), coefficients)
    out = jax.ShapeDtypeStruct((per, 5 * groups * per), f32)
    return pl.pallas_call(
        split_kernel, out_shape=(out, out), in_specs=[vmem], out_specs=(vmem, vmem), name="split"
    )(band)


def solution(mesh):
    return jax.shard_map(
        functools.partial(local, mesh.shape["slab"], mesh.shape["grp"]),
        mesh=mesh,
        in_specs=(P("slab", None, None), P(("slab", "grp"), None, None, None), P(), P()),
        out_specs=(P(("slab", "grp"), None), P(("slab", "grp"), None)),
        check_vma=False,
    )
```

```python
import functools

import jax
import jax.numpy as jnp
import numpy as np
from jax import lax
from jax.experimental import pallas as pl
from jax.experimental.pallas import tpu as pltpu
from jax.sharding import PartitionSpec as P

COMP = 8
CX = 32
CY = 32
BLOCK = 256
LANES = 128
MESH = pl.DeviceIdType.MESH
PAIRS = ((0, 3), (1, 2))
SHORT = (0, 3, 1, 2)


def haar_signs():
    ids = np.arange(COMP)
    common = ids[:, None] & ids[None, :]
    parity = (common % 2 + common // 2 % 2 + common // 4 % 2) % 2
    return (1 - 2 * parity).astype(np.float32)


def matrices(rows):
    haar = np.einsum("kc,mn->kmnc", haar_signs(), np.eye(rows, dtype=np.float32))
    haar = haar.reshape(COMP * rows, rows * COMP)
    lap = np.zeros((BLOCK, BLOCK), np.float32)
    for i in range(BLOCK):
        if i % CY:
            lap[i - 1, i] = lap[i, i - 1] = -0.5
        if i >= CY:
            lap[i - CY, i] = lap[i, i - CY] = -0.5
    return jnp.asarray(haar, jnp.bfloat16), jnp.asarray(lap, jnp.bfloat16)


def band_kernel(
    slabs,
    groups,
    depth,
    pot_hbm,
    center_hbm,
    extent_hbm,
    haar_hbm,
    lap_hbm,
    coef_hbm,
    out_ref,
    pot_ref,
    center_ref,
    extent_ref,
    haar_ref,
    lap_ref,
    coef,
    frames,
    raw,
    far,
    orb,
    rest,
    pot,
    pot_out,
    pot_in,
    limits,
    acc,
    place,
    rows,
    got_rows,
    load_sem,
    sent_sem,
    pot_recv,
    outer_recv,
    main_recv,
    far_recv,
    rows_recv,
):
    f32, bf16 = jnp.float32, jnp.bfloat16
    slab = lax.axis_index("slab")
    me = lax.axis_index("grp")
    per, box, comp, cells = coef.shape
    half = depth // 2
    team = 2 * groups
    rows_tile = 4 * per
    odd = lax.rem(slab, 2)
    base = slab - odd
    mine = odd * groups + me
    ahead = lax.rem(slab + 2, slabs)
    behind = lax.rem(slab + slabs - 2, slabs)

    def mate(step):
        low, scale, rest_of, bits = 0, 1, me, step
        while scale < groups:
            bit = lax.rem(rest_of, 2)
            rest_of = rest_of // 2
            low = low + scale * (1 - bit if bits % 2 else bit)
            bits //= 2
            scale *= 2
        par = 1 - odd if bits else odd
        return par, low

    steps = [6, 2, 4, 7, 3, 5, 1, 0]

    loads = [
        pltpu.make_async_copy(source, target, load_sem.at[n])
        for n, (source, target) in enumerate(
            (
                (center_hbm, center_ref),
                (extent_hbm, extent_ref),
                (coef_hbm, coef),
                (haar_hbm, haar_ref),
                (pot_hbm, pot_ref),
                (lap_hbm, lap_ref),
            )
        )
    ]
    for copy in loads:
        copy.start()

    barrier = pltpu.get_barrier_semaphore()
    for step in steps:
        if step:
            par, low = mate(step)
            pl.semaphore_signal(
                barrier, inc=1, device_id=(base + par, low), device_id_type=MESH
            )
    for place_at in (ahead, behind):
        pl.semaphore_signal(barrier, inc=1, device_id=(place_at, me), device_id_type=MESH)

    def push(kind, source, target, recv, to):
        copy = pltpu.make_async_remote_copy(
            src_ref=source,
            dst_ref=target,
            send_sem=sent_sem.at[kind],
            recv_sem=recv,
            device_id=to,
            device_id_type=MESH,
        )
        copy.start()

    def arrive(block, sem):
        pltpu.make_async_copy(block, block, sem).wait()

    def iota(shape, dim):
        return lax.broadcasted_iota(jnp.int32, shape, dim)

    def plane_of(row):
        pair = row // 8
        first = jnp.where(pair == 1, 3, jnp.where(pair == 2, 1, jnp.where(pair == 3, 2, 0)))
        return first + half * (lax.rem(row, 8) // per)

    row8 = iota((8, LANES), 0)
    func = lax.rem(row8, per)
    upper = row8 // per

    def spread(values):
        vec = jnp.full((8, LANES), values[0], jnp.int32)
        for f in range(1, per):
            vec = jnp.where(func == f, values[f], vec)
        return vec

    loads[0].wait()
    loads[1].wait()
    first = (slab * groups + me) * per
    extents = [extent_ref[first + f] for f in range(per)]
    starts = [
        center_ref[first + f] - slab * depth - lax.shift_right_logical(extents[f], 1)
        for f in range(per)
    ]
    start_rows, end_rows = spread(starts), spread([s + e for s, e in zip(starts, extents)])

    def build(index, outer, pairs):
        planes, masks = [], []
        for i in pairs:
            for h in range(2):
                for f in range(per):
                    j = i + half * h
                    away = j + depth - starts[f]
                    away = jnp.where(away < extents[f], away, away - 2 * depth)
                    near = j - starts[f]
                    if j == depth - 1:
                        p = odd * (near if outer else away)
                        p += (1 - odd) * (away if outer else near)
                    else:
                        p = away if outer else near
                    planes.append(coef[f, jnp.clip(p, 0, box - 1)].astype(f32))
            j = i + half * upper
            away = (j < end_rows - depth) | (j >= start_rows + depth)
            near = (j >= start_rows) & (j < end_rows)
            traded = (j == depth - 1) & (odd == 1)
            masks.append(jnp.where(traded != outer, away.astype(jnp.int32), near.astype(jnp.int32)) == 1)
        stacked = jnp.concatenate(planes, 0).astype(bf16)
        fine = jnp.dot(haar_ref[...], stacked, preferred_element_type=f32)
        keep = jnp.concatenate(masks, 0)
        for k in range(comp):
            for v in range(cells // LANES):
                at = slice(v * LANES, (v + 1) * LANES)
                part = fine[k * rows_tile : (k + 1) * rows_tile, at]
                frames[index, k, :, at] = jnp.where(keep, part, 0.0).astype(bf16)

    def tile_target(index, par, low):
        if index in (0, 3):
            return orb.at[par, index // 3, (1 + par) * groups + low]
        return raw.at[index - 1, par * groups + low]

    def arrive_main(index):
        arrive(frames.at[0], main_recv.at[index])

    def piece(ref, part):
        return ref if part is None else ref.at[:, part * cells // 2 : (part + 1) * cells // 2]

    def send_tiles(index, part=None):
        for step in steps:
            par, low = mate(step)
            source = piece(frames.at[index, par * groups + low], part)
            target = piece(tile_target(index, odd, me), part)
            if index in (0, 3):
                recv = main_recv.at[index // 3]
            else:
                recv = outer_recv.at[2 * index - 2 if part is None else part, mine]
            if step:
                push(0, source, target, recv, (base + par, low))
            else:
                pltpu.make_async_copy(source, target, recv).start()

    urgent = base // 2 // ((slabs + 2) // 4)
    own_first = 1 - lax.rem(urgent + odd, 2)

    row_wide = iota((8, cells), 0)

    def relay(index, place, part=None):
        if place < 2:
            par, low = mate(place)
        else:
            own = place - 2 < 2, place - 2 >= 4
            par = odd + (1 - 2 * odd) * (1 - (own[0] * own_first + own[1] * (1 - own_first)))
            first = mate((2, 3, 0, 1, 2, 3)[place - 2])[1]
            second = mate((0, 1, 2, 3, 2, 3)[place - 2])[1]
            low = own_first * first + (1 - own_first) * second
        if place:
            block = piece(tile_target(index, par, low), part)
            row = 2 * index - 2 if part is None else part
            arrive(block, outer_recv.at[row, par * groups + low])
        else:
            block = piece(frames.at[index, mine], part)
        push(
            1,
            block,
            piece(far.at[1 - par, (index - 1) * groups + low], part),
            far_recv.at[1 - par],
            (lax.rem(slab + slabs + 4 * par - 2, slabs), me),
        )

    loads[2].wait()
    loads[3].wait()
    build(1, True, PAIRS[1])
    pl.semaphore_wait(barrier, team + 1)
    send_tiles(1, 0)
    send_tiles(1, 1)
    relay(1, 0)
    build(2, True, PAIRS[0])
    relay(2, 0)
    send_tiles(2)
    relay(1, 1, 0)
    relay(1, 1, 1)
    loads[4].wait()
    loads[5].wait()
    theirs = (1 - odd) * groups + me
    own_pot = pot_ref[...].astype(f32).reshape(depth * comp, cells).astype(bf16)
    at_plane, at_column = iota((16, depth * comp), 0), iota((16, depth * comp), 1)
    pick = jnp.where(at_column == at_plane * comp + theirs, 1.0, 0.0).astype(bf16)
    sent = jnp.dot(pick, own_pot, preferred_element_type=f32)
    pot_out[...] = sent[:depth].astype(bf16)
    at_row, at_column = iota((4 * depth, depth * comp), 0), iota((4 * depth, depth * comp), 1)
    pick = jnp.where(at_column == plane_of(at_row) * comp + mine, 1.0, 0.0).astype(bf16)
    pot[odd] = jnp.dot(pick, own_pot, preferred_element_type=f32)

    push(2, pot_out, pot_in, pot_recv, (base + 1 - odd, me))
    build(0, False, PAIRS[0])
    send_tiles(0)

    build(3, False, PAIRS[1])
    send_tiles(3)
    relay(2, 1)

    for slot in range(4):
        home = lax.rem(base + slabs - 1 + slot, slabs)
        for g in range(groups):
            at = (home * groups + g) * per
            ext = [extent_ref[at + f] for f in range(per)]
            begin = [
                center_ref[at + f] - home * depth - lax.shift_right_logical(ext[f], 1)
                for f in range(per)
            ]
            limits[slot, g, 0] = spread(begin)
            limits[slot, g, 1] = spread([b + e for b, e in zip(begin, ext)])

    at_row, at_column = iota((2 * LANES, LANES), 0), iota((2 * LANES, LANES), 1)
    lane = lax.rem(at_row, LANES)
    slot_of = lane // 64 + 2 * (lax.rem(lane, 8 * 2) // 8)
    member = lax.rem(lane, 64) // 16 * per + lax.rem(lane, per)
    near = at_row < LANES
    band = jnp.where(near, slot_of + 1 - odd, slot_of - 1 + 3 * odd)
    fits = (band >= 0) & (band < 5) & (at_column == band * groups * per + member)
    place[...] = jnp.where(fits, 1.0, 0.0)

    low_half = row8 < per
    lane8 = iota((8, LANES), 1)
    vregs = cells // LANES
    blocks = cells // BLOCK
    per_block = BLOCK // LANES

    def split(ref):
        wide = ref[...].astype(f32)
        cut = lambda part: [part[:, v * LANES : (v + 1) * LANES] for v in range(vregs)]
        return cut(wide[:8]), cut(wide[8:])

    for part in range(2):
        for turn in range(2, 8):
            relay(1, turn, part)
    for turn in range(2, 8):
        relay(2, turn)
    arrive_main(0)
    for part in range(2):
        arrive(piece(tile_target(1, odd, me), part), outer_recv.at[part, mine])
    arrive(tile_target(2, odd, me), outer_recv.at[2, mine])
    arrive(pot_in, pot_recv)
    padded = jnp.concatenate([pot_in[...].astype(f32), jnp.zeros((depth, cells), f32)], 0)
    at_row, at_column = iota((4 * depth, 2 * depth), 0), iota((4 * depth, 2 * depth), 1)
    pick = jnp.where(at_column == plane_of(at_row), 1.0, 0.0).astype(bf16)
    pot[1 - odd] = jnp.dot(pick, padded.astype(bf16), preferred_element_type=f32)

    def swap(low_rows, high_rows):
        return [
            pltpu.roll(jnp.where(low_half, a, b), per, 0) for a, b in zip(low_rows, high_rows)
        ]

    def select(keep, rows_in):
        return [jnp.where(keep, x, 0.0) for x in rows_in]

    def finish(side, at, planes, before, after, keeps):
        tiles = [orb.at[side, t, at] for t in range(2)]
        stack = []
        for q in range(blocks):
            for t in range(2):
                stack.append(tiles[t][:, q * BLOCK : (q + 1) * BLOCK])
        beside = jnp.dot(jnp.concatenate(stack, 0), lap_ref[...], preferred_element_type=f32)
        shifted = [before, *planes, after]
        for v in range(vregs):
            done = {}
            q, part = divmod(v, per_block)
            for n, i in enumerate(SHORT):
                total = shifted[i][v] + shifted[i + 2][v]
                if part == 0 and v:
                    moved = pltpu.roll(planes[i][v - 1], CY, 1)
                    total = total + jnp.where(lane8 < CY, moved, 0.0)
                if part == per_block - 1 and v < vregs - 1:
                    moved = pltpu.roll(planes[i][v + 1], LANES - CY, 1)
                    total = total + jnp.where(lane8 >= LANES - CY, moved, 0.0)
                top = (q * 4 + n) * 8
                value = beside[top : top + 8, part * LANES : (part + 1) * LANES]
                value = value - 0.5 * total
                value = value + pot[side, n * 8 : n * 8 + 8, v * LANES : (v + 1) * LANES] * (
                    planes[i][v]
                )
                done[i] = jnp.where(keeps[i], value, 0.0)
            for t in range(2):
                both = jnp.concatenate([done[i] for i in PAIRS[t]], 0)
                rest[side, t, at, :, v * LANES : (v + 1) * LANES] = both.astype(bf16)

    def outer_frame(side, at, slot, g, up, below, above, first, second_tile):
        begin, end = limits[slot, g, 0], limits[slot, g, 1]
        low, high = (-box, end - depth) if up else (begin + depth, box)
        keeps = [
            (i + half * upper >= low) & (i + half * upper < high) for i in range(half)
        ]
        p0, p3 = first
        p1, p2 = split(second_tile)
        planes = [select(keeps[i], p) for i, p in enumerate((p0, p1, p2, p3))]
        for v in range(vregs):
            for t in range(2):
                both = jnp.concatenate([planes[i][v] for i in PAIRS[t]], 0)
                orb[side, t, at, :, v * LANES : (v + 1) * LANES] = both.astype(bf16)
        zero = [jnp.zeros((8, LANES), f32)] * vregs
        before, after = swap(planes[3], below or zero), swap(above or zero, planes[0])
        finish(side, at, planes, before, after, keeps)

    def main_frame(side, at, slot, g, up_tile, down_tile):
        begin, end = limits[slot, g, 0], limits[slot, g, 1]
        keeps = [
            (i + half * upper >= begin) & (i + half * upper < end) for i in range(half)
        ]
        p0, p3 = split(orb.at[side, 0, at])
        p1, p2 = split(orb.at[side, 1, at])
        planes = [p0, p1, p2, p3]
        out0, out3 = split(up_tile)[0], split(down_tile)[1]
        down3 = select(half - 1 + half * upper >= begin + depth, out3)
        up0 = select(half * upper < end - depth, out0)
        finish(side, at, planes, swap(p3, down3), swap(up0, p0), keeps)

    @pl.loop(0, groups)
    def _(g):
        edge = split(orb.at[0, 0, groups + g])[1]
        outer_frame(1, groups + g, 1, g, True, edge, None, split(raw.at[1, g]), raw.at[0, g])
        theirs = groups + g
        main0, main3 = split(orb.at[1, 0, groups + theirs])
        out0, out3 = split(raw.at[1, theirs])
        for v in range(vregs):
            both = jnp.concatenate([main0[v], jnp.where(low_half, main3[v], out3[v])], 0)
            orb[1, 0, groups + theirs, :, v * LANES : (v + 1) * LANES] = both.astype(bf16)
        out3 = [jnp.where(low_half, a, b) for a, b in zip(out3, main3)]
        outer_frame(
            0, groups + theirs, 2, g, False, None, main0, (out0, out3), raw.at[0, theirs]
        )

    quarter = lax.rem(lane8, 16) // per
    own_plane = [quarter == upper + 2 * pi for pi in range(2)]

    def own_planes(side, at, v):
        both = []
        for kind in range(2):
            top = (kind * count + at) * rows_tile
            lanes = slice(v * LANES, (v + 1) * LANES)
            value = jnp.where(own_plane[0], acc[side, top : top + 8, lanes], 0.0)
            both.append(value + jnp.where(own_plane[1], acc[side, top + 8 : top + 16, lanes], 0.0))
        return both

    def folded(both):
        margin, image = both
        value = jnp.where(low_half, margin, image)
        value += pltpu.roll(jnp.where(low_half, image, margin), per, 0)
        return value + pltpu.roll(value, LANES - 8, 1)

    left = lane8 < LANES // 2
    even = lax.rem(lane8, 16) < 8
    count = 3 * groups
    wide = count * rows_tile

    def limits_wide(slot, g):
        return jnp.concatenate([limits[slot, g, 0]] * vregs, 1)

    def far_frames(side):
        arrive(far.at[side], far_recv.at[side])
        for g in range(groups):
            first = split(far.at[side, groups + g])
            below = None if side else first[1]
            outer_frame(side, g, 3 * side, g, not side, below, None, first, far.at[side, g])

    def main_frames(side):
        for g in range(groups):
            at = (1 + side) * groups + g
            down = orb.at[0, 0, at] if side else raw.at[1, g]
            main_frame(side, at, 1 + side, g, raw.at[1, side * groups + g], down)

    def meet(side):
        for t in range(2):
            columns = orb[side, t].reshape(wide, cells)
            part = lax.dot_general(
                jnp.concatenate([columns, rest[side, t].reshape(wide, cells)], 0),
                columns,
                (((1,), (1,)), ((), ())),
                preferred_element_type=f32,
            )
            if t:
                acc[side, :, :wide] += part
            else:
                acc[side, :, :wide] = part
        for g in range(groups):
            one, two = folded(own_planes(side, g, 0)), folded(own_planes(side, g, 1))
            turned = pltpu.roll(one, LANES // 2, 1) if side else 0.0
            near_cols = jnp.where(left, 0.0, one) if side else one
            far_cols = jnp.where(left, two, turned)
            rows[3 * side, g] = jnp.where(even, near_cols, pltpu.roll(far_cols, 8, 1))

        for g in range(groups):
            push(
                3,
                rows.at[3 * side, g],
                got_rows.at[team + mine],
                rows_recv,
                (lax.rem(base + slabs - 1 + 3 * side, slabs), g),
            )

    def at_end(first):
        arrive_main(1)
        main_frames(first)
        far_frames(first)
        meet(first)
        main_frames(1 - first)
        far_frames(1 - first)
        meet(1 - first)

    def between():
        arrive_main(1)
        for side in range(2):
            main_frames(side)
        for side in range(2):
            far_frames(side)
            meet(side)

    pl.when(base == 0)(functools.partial(at_end, 0))
    pl.when(base == slabs - 2)(functools.partial(at_end, 1))
    pl.when((base > 0) & (base < slabs - 2))(between)

    tops = []
    for g in range(groups):
        plane0 = pltpu.roll(orb[0, 0, groups + g][:8].astype(f32), per, 0)
        here = (row_wide >= per) & (limits_wide(1, g) < 0)
        tops += [jnp.zeros((8, cells), f32), jnp.where(here, -0.5 * plane0, 0.0)]
    others = [far[0, groups + g] for g in range(groups)] + [raw[1, g] for g in range(groups)]
    top = (count + groups) * rows_tile
    acc[0, top : top + groups * rows_tile, :LANES] += lax.dot_general(
        jnp.concatenate(tops, 0).astype(bf16),
        jnp.concatenate(others, 0),
        (((1,), (1,)), ((), ())),
        preferred_element_type=f32,
    )
    for slot in (1, 2):
        for g in range(groups):
            at = slot * groups + g
            pair = [own_planes(side, at, 0) for side in range(2)]
            last = [own_planes(side, at, 1) for side in range(2)]
            near_cols = [jnp.where(left, v, v + w) for v, w in zip(*pair)]
            far_cols = [
                jnp.where(left, v + w, pltpu.roll(x, LANES // 2, 1))
                for v, w, x in zip(*last, pair[1])
            ]
            near_cols, far_cols = folded(near_cols), folded(far_cols)
            rows[slot, g] = jnp.where(even, near_cols, pltpu.roll(far_cols, 8, 1))
    for step in steps:
        par, low = mate(step)
        source, target = rows.at[1 + par, low], got_rows.at[mine]
        if step:
            push(3, source, target, rows_recv, (base + par, low))
        else:
            pltpu.make_async_copy(source, target, rows_recv).start()
    arrive(got_rows, rows_recv)
    sums = []
    for side in range(2):
        total = got_rows[side * team]
        for r in range(1, team):
            total = total + got_rows[side * team + r]
        sums.append(total)
    total = jnp.dot(
        jnp.concatenate(sums, 1),
        place[...],
        preferred_element_type=f32,
        precision=lax.Precision.HIGHEST,
    ) * (1.0 / comp)
    out_ref[...] = total + jnp.where(low_half, 0.0, 3.0 * pltpu.roll(total, per, 0))
    for kind, block in enumerate(
        (frames.at[:, : comp - 1], raw, pot_out, got_rows.at[: 2 * team - 1])
    ):
        arrive(block, sent_sem.at[kind])


def split_kernel(band_ref, margin_ref, ham_ref):
    per, width = margin_ref.shape
    margin_ref[...] = band_ref[:per, :width]
    ham_ref[...] = band_ref[per:, :width]


def local(slabs, groups, potential, coefficients, box_center, box_extent):
    per, box, comp, cells = coefficients.shape
    depth = potential.shape[0]
    team = 2 * groups
    rows_tile = 4 * per
    assert (depth, per, comp, groups) == (8, 4, team, 4)
    vmem = pl.BlockSpec(memory_space=pltpu.VMEM)
    anywhere = pl.BlockSpec(memory_space=pl.ANY)
    bf16, f32 = jnp.bfloat16, jnp.float32
    tiles = lambda *lead: pltpu.VMEM((*lead, rows_tile, cells), bf16)
    dma = pltpu.SemaphoreType.DMA
    band = pl.pallas_call(
        functools.partial(band_kernel, slabs, groups, depth),
        out_shape=jax.ShapeDtypeStruct((2 * per, LANES), f32),
        in_specs=[anywhere] * 6,
        out_specs=vmem,
        scratch_shapes=[
            pltpu.VMEM(potential.shape, bf16),
            pltpu.SMEM(box_center.shape, jnp.int32),
            pltpu.SMEM(box_extent.shape, jnp.int32),
            pltpu.VMEM((comp * rows_tile, comp * rows_tile), bf16),
            pltpu.VMEM((BLOCK, BLOCK), bf16),
            pltpu.VMEM((per, box, comp, cells), bf16),
            tiles(4, comp),
            tiles(2, team),
            tiles(2, 2 * groups),
            tiles(2, 2, 3 * groups),
            tiles(2, 2, 3 * groups),
            pltpu.VMEM((2, 4 * depth, cells), f32),
            pltpu.VMEM((depth, cells), bf16),
            pltpu.VMEM((depth, cells), bf16),
            pltpu.VMEM((4, groups, 2, 8, LANES), jnp.int32),
            pltpu.VMEM((2, 6 * groups * rows_tile, 2 * LANES), f32),
            pltpu.VMEM((2 * LANES, LANES), f32),
            pltpu.VMEM((4, groups, 2 * per, LANES), f32),
            pltpu.VMEM((2 * team, 2 * per, LANES), f32),
            dma((6,)),
            dma((4,)),
            dma,
            dma((3, team)),
            dma((2,)),
            dma((2,)),
            dma,
        ],
        compiler_params=pltpu.CompilerParams(collective_id=0, has_side_effects=True),
        name="band",
    )(potential, box_center, box_extent, *matrices(rows_tile), coefficients)
    out = jax.ShapeDtypeStruct((per, 5 * groups * per), f32)
    return pl.pallas_call(
        split_kernel, out_shape=(out, out), in_specs=[vmem], out_specs=(vmem, vmem), name="split"
    )(band)


def solution(mesh):
    return jax.shard_map(
        functools.partial(local, mesh.shape["slab"], mesh.shape["grp"]),
        mesh=mesh,
        in_specs=(P("slab", None, None), P(("slab", "grp"), None, None, None), P(), P()),
        out_specs=(P(("slab", "grp"), None), P(("slab", "grp"), None)),
        check_vma=False,
    )
```

```python
import functools

import jax
import jax.numpy as jnp
import numpy as np
from jax import lax
from jax.experimental import pallas as pl
from jax.experimental.pallas import tpu as pltpu
from jax.sharding import PartitionSpec as P

COMP = 8
CX = 32
CY = 32
BLOCK = 256
LANES = 128
MESH = pl.DeviceIdType.MESH
PAIRS = ((0, 3), (1, 2))
SHORT = (0, 3, 1, 2)


def haar_signs():
    ids = np.arange(COMP)
    common = ids[:, None] & ids[None, :]
    parity = (common % 2 + common // 2 % 2 + common // 4 % 2) % 2
    return (1 - 2 * parity).astype(np.float32)


def matrices(rows):
    haar = np.einsum("kc,mn->kmnc", haar_signs(), np.eye(rows, dtype=np.float32))
    haar = haar.reshape(COMP * rows, rows * COMP)
    lap = np.zeros((BLOCK, BLOCK), np.float32)
    for i in range(BLOCK):
        if i % CY:
            lap[i - 1, i] = lap[i, i - 1] = -0.5
        if i >= CY:
            lap[i - CY, i] = lap[i, i - CY] = -0.5
    return jnp.asarray(haar, jnp.bfloat16), jnp.asarray(lap, jnp.bfloat16)


def band_kernel(
    slabs,
    groups,
    depth,
    pot_hbm,
    center_hbm,
    extent_hbm,
    haar_hbm,
    lap_hbm,
    coef_hbm,
    out_ref,
    pot_ref,
    center_ref,
    extent_ref,
    haar_ref,
    lap_ref,
    coef,
    frames,
    raw,
    far,
    orb,
    rest,
    pot,
    pot_out,
    pot_in,
    limits,
    acc,
    place,
    rows,
    got_rows,
    owed,
    load_sem,
    sent_sem,
    pot_recv,
    outer_recv,
    main_recv,
    far_recv,
    rows_recv,
):
    f32, bf16 = jnp.float32, jnp.bfloat16
    slab = lax.axis_index("slab")
    me = lax.axis_index("grp")
    per, box, comp, cells = coef.shape
    half = depth // 2
    team = 2 * groups
    rows_tile = 4 * per
    odd = lax.rem(slab, 2)
    base = slab - odd
    mine = odd * groups + me
    ahead = lax.rem(slab + 2, slabs)
    behind = lax.rem(slab + slabs - 2, slabs)

    def mate(step):
        low, scale, rest_of, bits = 0, 1, me, step
        while scale < groups:
            bit = lax.rem(rest_of, 2)
            rest_of = rest_of // 2
            low = low + scale * (1 - bit if bits % 2 else bit)
            bits //= 2
            scale *= 2
        par = 1 - odd if bits else odd
        return par, low

    steps = [6, 2, 4, 7, 3, 5, 1, 0]

    loads = [
        pltpu.make_async_copy(source, target, load_sem.at[n])
        for n, (source, target) in enumerate(
            (
                (center_hbm, center_ref),
                (extent_hbm, extent_ref),
                (coef_hbm, coef),
                (haar_hbm, haar_ref),
                (pot_hbm, pot_ref),
                (lap_hbm, lap_ref),
            )
        )
    ]
    for copy in loads:
        copy.start()

    barrier = pltpu.get_barrier_semaphore()
    for step in steps:
        if step:
            par, low = mate(step)
            pl.semaphore_signal(
                barrier, inc=1, device_id=(base + par, low), device_id_type=MESH
            )
    for place_at in (ahead, behind):
        pl.semaphore_signal(barrier, inc=1, device_id=(place_at, me), device_id_type=MESH)

    def push(kind, source, target, recv, to):
        copy = pltpu.make_async_remote_copy(
            src_ref=source,
            dst_ref=target,
            send_sem=sent_sem.at[kind],
            recv_sem=recv,
            device_id=to,
            device_id_type=MESH,
        )
        copy.start()

    def arrive(block, sem):
        pltpu.make_async_copy(block, block, sem).wait()

    def iota(shape, dim):
        return lax.broadcasted_iota(jnp.int32, shape, dim)

    def plane_of(row):
        pair = row // 8
        first = jnp.where(pair == 1, 3, jnp.where(pair == 2, 1, jnp.where(pair == 3, 2, 0)))
        return first + half * (lax.rem(row, 8) // per)

    row8 = iota((8, LANES), 0)
    func = lax.rem(row8, per)
    upper = row8 // per

    def spread(values):
        vec = jnp.full((8, LANES), values[0], jnp.int32)
        for f in range(1, per):
            vec = jnp.where(func == f, values[f], vec)
        return vec

    loads[0].wait()
    loads[1].wait()
    first = (slab * groups + me) * per
    extents = [extent_ref[first + f] for f in range(per)]
    starts = [
        center_ref[first + f] - slab * depth - lax.shift_right_logical(extents[f], 1)
        for f in range(per)
    ]
    start_rows, end_rows = spread(starts), spread([s + e for s, e in zip(starts, extents)])

    def build(index, outer, pairs):
        planes, masks = [], []
        for i in pairs:
            for h in range(2):
                for f in range(per):
                    j = i + half * h
                    away = j + depth - starts[f]
                    away = jnp.where(away < extents[f], away, away - 2 * depth)
                    near = j - starts[f]
                    if j == depth - 1:
                        p = odd * (near if outer else away)
                        p += (1 - odd) * (away if outer else near)
                    else:
                        p = away if outer else near
                    planes.append(coef[f, jnp.clip(p, 0, box - 1)].astype(f32))
            j = i + half * upper
            away = (j < end_rows - depth) | (j >= start_rows + depth)
            near = (j >= start_rows) & (j < end_rows)
            traded = (j == depth - 1) & (odd == 1)
            masks.append(jnp.where(traded != outer, away.astype(jnp.int32), near.astype(jnp.int32)) == 1)
        stacked = jnp.concatenate(planes, 0).astype(bf16)
        fine = jnp.dot(haar_ref[...], stacked, preferred_element_type=f32)
        keep = jnp.concatenate(masks, 0)
        for k in range(comp):
            for v in range(cells // LANES):
                at = slice(v * LANES, (v + 1) * LANES)
                part = fine[k * rows_tile : (k + 1) * rows_tile, at]
                frames[index, k, :, at] = jnp.where(keep, part, 0.0).astype(bf16)

    def tile_target(index, par, low):
        if index in (0, 3):
            return orb.at[par, index // 3, (1 + par) * groups + low]
        return raw.at[index - 1, par * groups + low]

    def arrive_main(index):
        arrive(frames.at[0], main_recv.at[index])

    def piece(ref, part):
        return ref if part is None else ref.at[:, part * cells // 2 : (part + 1) * cells // 2]

    def send_tiles(index, part=None):
        for step in steps:
            par, low = mate(step)
            source = piece(frames.at[index, par * groups + low], part)
            target = piece(tile_target(index, odd, me), part)
            if index in (0, 3):
                recv = main_recv.at[index // 3]
            else:
                recv = outer_recv.at[2 * index - 2 if part is None else part, mine]
            if step:
                push(0, source, target, recv, (base + par, low))
            else:
                pltpu.make_async_copy(source, target, recv).start()

    urgent = base // 2 // ((slabs + 2) // 4)
    own_first = 1 - lax.rem(urgent + odd, 2)

    row_wide = iota((8, cells), 0)

    def relay(index, place, part=None):
        if place < 2:
            par, low = mate(place)
        else:
            own = place - 2 < 2, place - 2 >= 4
            par = odd + (1 - 2 * odd) * (1 - (own[0] * own_first + own[1] * (1 - own_first)))
            first = mate((2, 3, 0, 1, 2, 3)[place - 2])[1]
            second = mate((0, 1, 2, 3, 2, 3)[place - 2])[1]
            low = own_first * first + (1 - own_first) * second
        if place:
            block = piece(tile_target(index, par, low), part)
            row = 2 * index - 2 if part is None else part
            arrive(block, outer_recv.at[row, par * groups + low])
        else:
            block = piece(frames.at[index, mine], part)
        push(
            1,
            block,
            piece(far.at[1 - par, (index - 1) * groups + low], part),
            far_recv.at[1 - par],
            (lax.rem(slab + slabs + 4 * par - 2, slabs), me),
        )

    loads[2].wait()
    loads[3].wait()
    build(1, True, PAIRS[1])
    pl.semaphore_wait(barrier, team + 1)
    send_tiles(1, 0)
    send_tiles(1, 1)
    relay(1, 0)
    build(2, True, PAIRS[0])
    relay(2, 0)
    send_tiles(2)
    relay(1, 1, 0)
    relay(1, 1, 1)
    loads[4].wait()
    loads[5].wait()
    theirs = (1 - odd) * groups + me
    own_pot = pot_ref[...].astype(f32).reshape(depth * comp, cells).astype(bf16)
    at_plane, at_column = iota((16, depth * comp), 0), iota((16, depth * comp), 1)
    pick = jnp.where(at_column == at_plane * comp + theirs, 1.0, 0.0).astype(bf16)
    sent = jnp.dot(pick, own_pot, preferred_element_type=f32)
    pot_out[...] = sent[:depth].astype(bf16)
    at_row, at_column = iota((4 * depth, depth * comp), 0), iota((4 * depth, depth * comp), 1)
    pick = jnp.where(at_column == plane_of(at_row) * comp + mine, 1.0, 0.0).astype(bf16)
    pot[odd] = jnp.dot(pick, own_pot, preferred_element_type=f32)

    push(2, pot_out, pot_in, pot_recv, (base + 1 - odd, me))
    build(0, False, PAIRS[0])
    send_tiles(0)

    build(3, False, PAIRS[1])
    send_tiles(3)
    relay(2, 1)

    for slot in range(4):
        home = lax.rem(base + slabs - 1 + slot, slabs)
        for g in range(groups):
            at = (home * groups + g) * per
            ext = [extent_ref[at + f] for f in range(per)]
            begin = [
                center_ref[at + f] - home * depth - lax.shift_right_logical(ext[f], 1)
                for f in range(per)
            ]
            limits[slot, g, 0] = spread(begin)
            limits[slot, g, 1] = spread([b + e for b, e in zip(begin, ext)])

    at_row, at_column = iota((2 * LANES, LANES), 0), iota((2 * LANES, LANES), 1)
    lane = lax.rem(at_row, LANES)
    slot_of = lane // 64 + 2 * (lax.rem(lane, 8 * 2) // 8)
    member = lax.rem(lane, 64) // 16 * per + lax.rem(lane, per)
    near = at_row < LANES
    band = jnp.where(near, slot_of + 1 - odd, slot_of - 1 + 3 * odd)
    fits = (band >= 0) & (band < 5) & (at_column == band * groups * per + member)
    place[...] = jnp.where(fits, 1.0, 0.0)

    low_half = row8 < per
    lane8 = iota((8, LANES), 1)
    vregs = cells // LANES
    blocks = cells // BLOCK
    per_block = BLOCK // LANES

    def split(ref):
        wide = ref[...].astype(f32)
        cut = lambda part: [part[:, v * LANES : (v + 1) * LANES] for v in range(vregs)]
        return cut(wide[:8]), cut(wide[8:])

    for part in range(2):
        for turn in range(2, 8):
            relay(1, turn, part)
    for turn in range(2, 8):
        relay(2, turn)
    def lane_tiles(wide):
        return [wide[:, v * LANES : (v + 1) * LANES] for v in range(vregs)]

    def squares(n, exact):
        for f in range(per):
            value = coef[f, n].astype(f32)
            value = functools.reduce(jnp.add, lane_tiles(value * value))
            inside = jnp.full((8, LANES), n, jnp.int32) < extents[f]
            exact = exact[:f] + [exact[f] + jnp.where(inside, value, 0.0)] + exact[f + 1 :]
        return exact

    def fine_squares(n, rounded):
        for index in range(4):
            for top in (0, 8):
                value = frames[index, n, top : top + 8].astype(f32)
                rounded = rounded + functools.reduce(jnp.add, lane_tiles(value * value))
        return rounded

    zeros = jnp.zeros((8, LANES), f32)
    exact = lax.fori_loop(0, box, squares, [zeros] * per)
    rounded = lax.fori_loop(0, comp, fine_squares, zeros)
    lost = jnp.sum(rounded, axis=1, keepdims=True) * (-1.0 / comp)
    lost = lost + pltpu.roll(jnp.broadcast_to(lost, (8, LANES)), per, 0)
    for f in range(per):
        lost = lost + jnp.where(row8 == f, jnp.sum(exact[f]), 0.0)
    at_home = lane8 == 2 * groups * per + me * per + row8
    owed[...] = jnp.where((row8 < per) & at_home, lost, 0.0)

    arrive_main(0)
    for part in range(2):
        arrive(piece(tile_target(1, odd, me), part), outer_recv.at[part, mine])
    arrive(tile_target(2, odd, me), outer_recv.at[2, mine])
    arrive(pot_in, pot_recv)
    padded = jnp.concatenate([pot_in[...].astype(f32), jnp.zeros((depth, cells), f32)], 0)
    at_row, at_column = iota((4 * depth, 2 * depth), 0), iota((4 * depth, 2 * depth), 1)
    pick = jnp.where(at_column == plane_of(at_row), 1.0, 0.0).astype(bf16)
    pot[1 - odd] = jnp.dot(pick, padded.astype(bf16), preferred_element_type=f32)

    def swap(low_rows, high_rows):
        return [
            pltpu.roll(jnp.where(low_half, a, b), per, 0) for a, b in zip(low_rows, high_rows)
        ]

    def select(keep, rows_in):
        return [jnp.where(keep, x, 0.0) for x in rows_in]

    def finish(side, at, planes, before, after, keeps):
        tiles = [orb.at[side, t, at] for t in range(2)]
        stack = []
        for q in range(blocks):
            for t in range(2):
                stack.append(tiles[t][:, q * BLOCK : (q + 1) * BLOCK])
        beside = jnp.dot(jnp.concatenate(stack, 0), lap_ref[...], preferred_element_type=f32)
        shifted = [before, *planes, after]
        for v in range(vregs):
            done = {}
            q, part = divmod(v, per_block)
            for n, i in enumerate(SHORT):
                total = shifted[i][v] + shifted[i + 2][v]
                if part == 0 and v:
                    moved = pltpu.roll(planes[i][v - 1], CY, 1)
                    total = total + jnp.where(lane8 < CY, moved, 0.0)
                if part == per_block - 1 and v < vregs - 1:
                    moved = pltpu.roll(planes[i][v + 1], LANES - CY, 1)
                    total = total + jnp.where(lane8 >= LANES - CY, moved, 0.0)
                top = (q * 4 + n) * 8
                value = beside[top : top + 8, part * LANES : (part + 1) * LANES]
                value = value - 0.5 * total
                value = value + pot[side, n * 8 : n * 8 + 8, v * LANES : (v + 1) * LANES] * (
                    planes[i][v]
                )
                done[i] = jnp.where(keeps[i], value, 0.0)
            for t in range(2):
                both = jnp.concatenate([done[i] for i in PAIRS[t]], 0)
                rest[side, t, at, :, v * LANES : (v + 1) * LANES] = both.astype(bf16)

    def outer_frame(side, at, slot, g, up, below, above, first, second_tile):
        begin, end = limits[slot, g, 0], limits[slot, g, 1]
        low, high = (-box, end - depth) if up else (begin + depth, box)
        keeps = [
            (i + half * upper >= low) & (i + half * upper < high) for i in range(half)
        ]
        p0, p3 = first
        p1, p2 = split(second_tile)
        planes = [select(keeps[i], p) for i, p in enumerate((p0, p1, p2, p3))]
        for v in range(vregs):
            for t in range(2):
                both = jnp.concatenate([planes[i][v] for i in PAIRS[t]], 0)
                orb[side, t, at, :, v * LANES : (v + 1) * LANES] = both.astype(bf16)
        zero = [jnp.zeros((8, LANES), f32)] * vregs
        before, after = swap(planes[3], below or zero), swap(above or zero, planes[0])
        finish(side, at, planes, before, after, keeps)

    def main_frame(side, at, slot, g, up_tile, down_tile):
        begin, end = limits[slot, g, 0], limits[slot, g, 1]
        keeps = [
            (i + half * upper >= begin) & (i + half * upper < end) for i in range(half)
        ]
        p0, p3 = split(orb.at[side, 0, at])
        p1, p2 = split(orb.at[side, 1, at])
        planes = [p0, p1, p2, p3]
        out0, out3 = split(up_tile)[0], split(down_tile)[1]
        down3 = select(half - 1 + half * upper >= begin + depth, out3)
        up0 = select(half * upper < end - depth, out0)
        finish(side, at, planes, swap(p3, down3), swap(up0, p0), keeps)

    @pl.loop(0, groups)
    def _(g):
        edge = split(orb.at[0, 0, groups + g])[1]
        outer_frame(1, groups + g, 1, g, True, edge, None, split(raw.at[1, g]), raw.at[0, g])
        theirs = groups + g
        main0, main3 = split(orb.at[1, 0, groups + theirs])
        out0, out3 = split(raw.at[1, theirs])
        for v in range(vregs):
            both = jnp.concatenate([main0[v], jnp.where(low_half, main3[v], out3[v])], 0)
            orb[1, 0, groups + theirs, :, v * LANES : (v + 1) * LANES] = both.astype(bf16)
        out3 = [jnp.where(low_half, a, b) for a, b in zip(out3, main3)]
        outer_frame(
            0, groups + theirs, 2, g, False, None, main0, (out0, out3), raw.at[0, theirs]
        )

    quarter = lax.rem(lane8, 16) // per
    own_plane = [quarter == upper + 2 * pi for pi in range(2)]

    def own_planes(side, at, v):
        both = []
        for kind in range(2):
            top = (kind * count + at) * rows_tile
            lanes = slice(v * LANES, (v + 1) * LANES)
            value = jnp.where(own_plane[0], acc[side, top : top + 8, lanes], 0.0)
            both.append(value + jnp.where(own_plane[1], acc[side, top + 8 : top + 16, lanes], 0.0))
        return both

    def folded(both):
        margin, image = both
        value = jnp.where(low_half, margin, image)
        value += pltpu.roll(jnp.where(low_half, image, margin), per, 0)
        return value + pltpu.roll(value, LANES - 8, 1)

    left = lane8 < LANES // 2
    even = lax.rem(lane8, 16) < 8
    count = 3 * groups
    wide = count * rows_tile

    def limits_wide(slot, g):
        return jnp.concatenate([limits[slot, g, 0]] * vregs, 1)

    def far_frames(side):
        arrive(far.at[side], far_recv.at[side])
        for g in range(groups):
            first = split(far.at[side, groups + g])
            below = None if side else first[1]
            outer_frame(side, g, 3 * side, g, not side, below, None, first, far.at[side, g])

    def main_frames(side):
        for g in range(groups):
            at = (1 + side) * groups + g
            down = orb.at[0, 0, at] if side else raw.at[1, g]
            main_frame(side, at, 1 + side, g, raw.at[1, side * groups + g], down)

    def meet(side):
        for t in range(2):
            columns = orb[side, t].reshape(wide, cells)
            part = lax.dot_general(
                jnp.concatenate([columns, rest[side, t].reshape(wide, cells)], 0),
                columns,
                (((1,), (1,)), ((), ())),
                preferred_element_type=f32,
            )
            if t:
                acc[side, :, :wide] += part
            else:
                acc[side, :, :wide] = part
        for g in range(groups):
            one, two = folded(own_planes(side, g, 0)), folded(own_planes(side, g, 1))
            turned = pltpu.roll(one, LANES // 2, 1) if side else 0.0
            near_cols = jnp.where(left, 0.0, one) if side else one
            far_cols = jnp.where(left, two, turned)
            rows[3 * side, g] = jnp.where(even, near_cols, pltpu.roll(far_cols, 8, 1))

        for g in range(groups):
            push(
                3,
                rows.at[3 * side, g],
                got_rows.at[team + mine],
                rows_recv,
                (lax.rem(base + slabs - 1 + 3 * side, slabs), g),
            )

    def at_end(first):
        arrive_main(1)
        main_frames(first)
        far_frames(first)
        meet(first)
        main_frames(1 - first)
        far_frames(1 - first)
        meet(1 - first)

    def between():
        arrive_main(1)
        for side in range(2):
            main_frames(side)
        for side in range(2):
            far_frames(side)
            meet(side)

    pl.when(base == 0)(functools.partial(at_end, 0))
    pl.when(base == slabs - 2)(functools.partial(at_end, 1))
    pl.when((base > 0) & (base < slabs - 2))(between)

    tops = []
    for g in range(groups):
        plane0 = pltpu.roll(orb[0, 0, groups + g][:8].astype(f32), per, 0)
        here = (row_wide >= per) & (limits_wide(1, g) < 0)
        tops += [jnp.zeros((8, cells), f32), jnp.where(here, -0.5 * plane0, 0.0)]
    others = [far[0, groups + g] for g in range(groups)] + [raw[1, g] for g in range(groups)]
    top = (count + groups) * rows_tile
    acc[0, top : top + groups * rows_tile, :LANES] += lax.dot_general(
        jnp.concatenate(tops, 0).astype(bf16),
        jnp.concatenate(others, 0),
        (((1,), (1,)), ((), ())),
        preferred_element_type=f32,
    )
    for slot in (1, 2):
        for g in range(groups):
            at = slot * groups + g
            pair = [own_planes(side, at, 0) for side in range(2)]
            last = [own_planes(side, at, 1) for side in range(2)]
            near_cols = [jnp.where(left, v, v + w) for v, w in zip(*pair)]
            far_cols = [
                jnp.where(left, v + w, pltpu.roll(x, LANES // 2, 1))
                for v, w, x in zip(*last, pair[1])
            ]
            near_cols, far_cols = folded(near_cols), folded(far_cols)
            rows[slot, g] = jnp.where(even, near_cols, pltpu.roll(far_cols, 8, 1))
    for step in steps:
        par, low = mate(step)
        source, target = rows.at[1 + par, low], got_rows.at[mine]
        if step:
            push(3, source, target, rows_recv, (base + par, low))
        else:
            pltpu.make_async_copy(source, target, rows_recv).start()
    arrive(got_rows, rows_recv)
    sums = []
    for side in range(2):
        total = got_rows[side * team]
        for r in range(1, team):
            total = total + got_rows[side * team + r]
        sums.append(total)
    total = jnp.dot(
        jnp.concatenate(sums, 1),
        place[...],
        preferred_element_type=f32,
        precision=lax.Precision.HIGHEST,
    ) * (1.0 / comp) + owed[...]
    out_ref[...] = total + jnp.where(low_half, 0.0, 3.0 * pltpu.roll(total, per, 0))
    for kind, block in enumerate(
        (frames.at[:, : comp - 1], raw, pot_out, got_rows.at[: 2 * team - 1])
    ):
        arrive(block, sent_sem.at[kind])


def split_kernel(band_ref, margin_ref, ham_ref):
    per, width = margin_ref.shape
    margin_ref[...] = band_ref[:per, :width]
    ham_ref[...] = band_ref[per:, :width]


def local(slabs, groups, potential, coefficients, box_center, box_extent):
    per, box, comp, cells = coefficients.shape
    depth = potential.shape[0]
    team = 2 * groups
    rows_tile = 4 * per
    assert (depth, per, comp, groups) == (8, 4, team, 4)
    vmem = pl.BlockSpec(memory_space=pltpu.VMEM)
    anywhere = pl.BlockSpec(memory_space=pl.ANY)
    bf16, f32 = jnp.bfloat16, jnp.float32
    tiles = lambda *lead: pltpu.VMEM((*lead, rows_tile, cells), bf16)
    dma = pltpu.SemaphoreType.DMA
    band = pl.pallas_call(
        functools.partial(band_kernel, slabs, groups, depth),
        out_shape=jax.ShapeDtypeStruct((2 * per, LANES), f32),
        in_specs=[anywhere] * 6,
        out_specs=vmem,
        scratch_shapes=[
            pltpu.VMEM(potential.shape, bf16),
            pltpu.SMEM(box_center.shape, jnp.int32),
            pltpu.SMEM(box_extent.shape, jnp.int32),
            pltpu.VMEM((comp * rows_tile, comp * rows_tile), bf16),
            pltpu.VMEM((BLOCK, BLOCK), bf16),
            pltpu.VMEM((per, box, comp, cells), bf16),
            tiles(4, comp),
            tiles(2, team),
            tiles(2, 2 * groups),
            tiles(2, 2, 3 * groups),
            tiles(2, 2, 3 * groups),
            pltpu.VMEM((2, 4 * depth, cells), f32),
            pltpu.VMEM((depth, cells), bf16),
            pltpu.VMEM((depth, cells), bf16),
            pltpu.VMEM((4, groups, 2, 8, LANES), jnp.int32),
            pltpu.VMEM((2, 6 * groups * rows_tile, 2 * LANES), f32),
            pltpu.VMEM((2 * LANES, LANES), f32),
            pltpu.VMEM((4, groups, 2 * per, LANES), f32),
            pltpu.VMEM((2 * team, 2 * per, LANES), f32),
            pltpu.VMEM((2 * per, LANES), f32),
            dma((6,)),
            dma((4,)),
            dma,
            dma((3, team)),
            dma((2,)),
            dma((2,)),
            dma,
        ],
        compiler_params=pltpu.CompilerParams(collective_id=0, has_side_effects=True),
        name="band",
    )(potential, box_center, box_extent, *matrices(rows_tile), coefficients)
    out = jax.ShapeDtypeStruct((per, 5 * groups * per), f32)
    return pl.pallas_call(
        split_kernel, out_shape=(out, out), in_specs=[vmem], out_specs=(vmem, vmem), name="split"
    )(band)


def solution(mesh):
    return jax.shard_map(
        functools.partial(local, mesh.shape["slab"], mesh.shape["grp"]),
        mesh=mesh,
        in_specs=(P("slab", None, None), P(("slab", "grp"), None, None, None), P(), P()),
        out_specs=(P(("slab", "grp"), None), P(("slab", "grp"), None)),
        check_vma=False,
    )
```
